256 devices in a mesh: tgt: 16 (over z_hi, y, core), src: 16 (over z_lo, x).
Axes of the slice: x: 4, y: 4, z: 8 (z_hi: 2, z_lo: 4; z = z_hi * 4 + z_lo), core: 2. Of those that a mesh axis runs over, the one named last changes fastest.
Arguments:
- targets: bfloat16 [64, 64, 4096], P('tgt', 'src'), may hold values from -6 to 6
- sources: bfloat16 [16, 64, 4096], P('src', 'tgt'), may hold values from -6 to 6
- exponents: float32 [8], replicated, may hold values from 0.005 to 0.76
- coefficients: float32 [8], replicated, may hold values from -0.08 to 0.08
Outputs:
- exchange: float32 [64, 64, 4096], P('src', 'tgt')
The draws below stay inside these ranges and needn't reach their ends.
All inputs are finite; a program needn't handle non-finite values.
Results may differ from the reference program's by a relative error of at most 0.0063.
The reference program's roundings to bfloat16 on the way count: a program that leaves them out, or rounds other values in their place, can miss the bound.
Values may be sent and summed in bfloat16 or wider, within the bound.
No kernel may reach another device: no remote copies, remote signals or barrier semaphores. Data moves between devices by JAX's collectives and lax.ppermute only.
A program may use at most 64 MiB of HBM per device.

```python
import math
import jax
import jax.numpy as jnp
from jax import lax

G = 64
GAUSS = 8
NT = 64
NS = 16


def gauss_terms(key):
    base_key = jax.random.fold_in(key, 7301)
    jitter_key, weight_key, sign_key = jax.random.split(base_key, 3)
    offsets = jax.random.uniform(jitter_key, (GAUSS,), jnp.float32, 0.4, 0.6)
    levels = (jnp.arange(GAUSS, dtype=jnp.float32) + offsets) / GAUSS
    exponents = 0.004 * jnp.exp(levels * math.log(250.0))
    weights = jax.random.uniform(weight_key, (GAUSS,), jnp.float32, 0.6, 1.4)
    ordering = jax.random.permutation(sign_key, GAUSS)
    sign_flip = jnp.where(ordering < 3, -1.0, 1.0).astype(jnp.float32)
    coefficients = 0.08 * sign_flip * weights * jnp.power(2.0 * exponents / math.pi, 0.75)
    return (exponents.astype(jnp.float32), coefficients.astype(jnp.float32))


def draw_exponents(key, part):
    return gauss_terms(key)[0]


def draw_coefficients(key, part):
    return gauss_terms(key)[1]


def raised(drawn, key, source, target, blocks, factor):
    owner, partner = [(jnp.arange(drawn.shape[axis_at]) // (drawn.shape[axis_at] // blocks)).reshape([-1 if axis == axis_at else 1 for axis in range(drawn.ndim)]) for axis_at in (source, target)]
    chosen = jax.random.permutation(key, blocks)[partner]
    strong = (owner == chosen) | (owner == (partner + blocks // 2) % blocks)
    return jnp.where(strong, factor * drawn, drawn)


def shard_levels(rng, shape, pieces, least, largest):
    factor_of = 1.0
    for dim, shards_of in pieces:
        draws = jax.random.uniform(jax.random.fold_in(jax.random.fold_in(rng, 6), dim), (shards_of,), jnp.float32, least / len(pieces), largest / len(pieces))
        factor_of = factor_of * jnp.repeat(jnp.exp(draws), shape[dim] // shards_of).reshape((-1,) + (1,) * (len(shape) - 1 - dim))
    return factor_of


def bell_draw(stream_key, dims, width, reach, shards=(), held_as=jnp.bfloat16):
    factor_of = shard_levels(stream_key, dims, shards, -0.22, 0.18) if shards else 1.0
    entries = jax.random.normal(stream_key, dims, jnp.float32) * width * factor_of
    return jnp.minimum(jnp.maximum(entries, -reach), reach).astype(held_as)


def noise_with(stream_key, dims, scale, limit, cuts, heavy, held_as=jnp.bfloat16):
    values = scale * jax.random.normal(stream_key, dims, jnp.float32)
    if cuts:
        values = values * shard_levels(stream_key, dims, cuts, -0.22, 0.18)
    return jnp.clip(raised(values, jax.random.fold_in(stream_key, 3), *heavy), -limit, limit).astype(held_as)


def setup_inputs(seed: int = 0) -> dict:
    key_of = jax.random.split(jax.random.key(seed), 5)
    targets = bell_draw(key_of[0], (NT, G, G * G), 1.0, 6.0, ((0, 16), (1, 16)))
    sources = noise_with(key_of[1], (NS, G, G * G), 1.0, 6.0, ((0, 16), (1, 16)), (0, 1, 16, 2.0))
    exponents = draw_exponents(jax.random.fold_in(key_of[4], 71), 0)
    coefficients = draw_coefficients(jax.random.fold_in(key_of[4], 71), 0)
    return dict(targets=targets, sources=sources, exponents=exponents, coefficients=coefficients)


def kernels(exponents, coefficients):
    grid_pos = jnp.arange(G, dtype=jnp.int32)
    distance = jnp.abs(grid_pos[:, None] - grid_pos[None, :])
    distance = jnp.minimum(distance, G - distance).astype(jnp.float32)
    gauss_table = jnp.exp(-exponents[:, None, None] * (distance * distance)[None])
    weighted = coefficients[:, None, None] * gauss_table
    return gauss_table.astype(jnp.bfloat16), weighted.astype(jnp.bfloat16)


def pair_term(target, source, kernel_table, weighted):
    density = (target.astype(jnp.float32) * source.astype(jnp.float32)).astype(jnp.bfloat16)
    density = lax.optimization_barrier(density).astype(jnp.float32)
    first_pass = jnp.einsum('gax,xm->gam', kernel_table.astype(jnp.float32), density).astype(jnp.bfloat16)
    first_pass = lax.optimization_barrier(first_pass).astype(jnp.float32).reshape(GAUSS, G, G, G)
    second_pass = jnp.einsum('gby,gayz->gabz', kernel_table.astype(jnp.float32), first_pass).astype(jnp.bfloat16)
    second_pass = lax.optimization_barrier(second_pass).astype(jnp.float32)
    potential = jnp.einsum('gcz,gabz->abc', weighted.astype(jnp.float32), second_pass).reshape(G, G * G)
    return potential * source.astype(jnp.float32)


def reference(targets, sources, exponents, coefficients):
    kernel_table, weighted = kernels(exponents, coefficients)

    def one_target(target):
        def add_source(summed, source):
            return summed + pair_term(target, source, kernel_table, weighted), None

        summed, _ = lax.scan(add_source, jnp.zeros((G, G * G), jnp.float32), sources)
        return -summed

    result = lax.map(one_target, targets)
    return jnp.transpose(result, (1, 0, 2))
```

```python
import functools

import jax
import jax.numpy as jnp
import numpy as np
from jax import lax
from jax.experimental import pallas as pl
from jax.experimental.pallas import tpu as pltpu
from jax.sharding import Mesh
from jax.sharding import PartitionSpec as P

G = 64
GAUSS = 8
BF16, F32 = jnp.bfloat16, jnp.float32

SCALE = {0: 1.0, 1: 1.869537353515625, 2: 1.62451171875, 4: 1.13287353515625, 8: 1.8672027587890625, 16: 1.0, 32: 1.0}


def basis():
    n = np.arange(G)
    waves = [(k, np.cos) for k in range(G // 2 + 1)] + [(k, np.sin) for k in range(1, G // 2)]
    rows = np.stack([SCALE[k & -k] * wave(2 * np.pi * k * n / G) for k, wave in waves])
    rows[np.abs(rows) < 1e-12] = 0
    return rows, np.array([k for k, _ in waves])


def basis_blocks():
    rows, _ = basis()
    parity = np.array([2 * r + h for h in range(2) for r in range(32)])
    z_in, y_in, x_in = rows.T, rows[:, parity], rows
    return [jnp.asarray(np.kron(np.eye(4), m), BF16) for m in (z_in, y_in, x_in, x_in.T, y_in.T, z_in.T)]


def spectrum(exponents, coefficients):
    rows, freq = basis()
    n = np.arange(G)
    distance = np.minimum(n, G - n).astype(np.float32)
    table = jnp.exp(-exponents[:, None] * (distance * distance)[None])
    weighted = (coefficients[:, None] * table).astype(BF16).astype(F32)
    table = table.astype(BF16).astype(F32)
    waves = jnp.asarray(np.cos(2 * np.pi * np.outer(n, freq) / G) / (rows * rows).sum(1)[None], F32)
    plain = jnp.dot(table, waves, precision=lax.Precision.HIGHEST)
    scaled = jnp.dot(weighted, waves, precision=lax.Precision.HIGHEST)
    scaled = jnp.concatenate([scaled, scaled], axis=1)
    total = 0
    for g in range(GAUSS):
        total = total + (plain[g][:, None] * plain[g][None, :])[:, :, None] * scaled[g][None, None, :]
    return total


def pair_kernel(*refs):
    t_in, s_in, d_ref = refs[:4], refs[4:12], refs[12]
    z_in, y_in, x_in, x_out, y_out, z_out = refs[13:19]
    outs = refs[19:23]
    t_all, s_all, s_rows, field, t_sem, s_sem = refs[23:]
    zh, y, c, zl, x = (lax.axis_index(a) for a in ("zh", "y", "c", "zl", "x"))

    t_copies, s_copies = [], []
    for j in range(4):
        for k in range(4):
            block = lax.rem(zl - k + 4, 4) * 4 + lax.rem(x - j + 4, 4)
            t_copies.append(pltpu.make_async_copy(t_in[j].at[k], t_all.at[block], t_sem.at[4 * j + k]))
    for i in range(4):
        for e in range(2):
            for q in range(8):
                high = lax.rem(zh * 4 + zl - q + 8, 8) // 4
                block = high * 8 + lax.rem(y - i + 4, 4) * 2 + (c if e == 0 else 1 - c)
                s_copies.append(
                    pltpu.make_async_copy(s_in[2 * i + e].at[q], s_all.at[q % 4, block], s_sem.at[(2 * i + e) * 8 + q])
                )
    for copy in t_copies + s_copies:
        copy.start()
    for copy in t_copies + s_copies:
        copy.wait()

    lane = lax.broadcasted_iota(jnp.int32, (4, 32, 128), 2) < 64

    def swap(a):
        return pltpu.roll(a, 64, 2)

    def enter(b, carry):
        target = t_all[b]
        turned = swap(target)
        target = jnp.concatenate([jnp.where(lane, target, turned), jnp.where(lane, turned, target)], axis=1)
        target = target.reshape(256, 128)
        dense = []
        for h in range(2):
            one, two = s_all[2 * h, b], s_all[2 * h + 1, b]
            source = jnp.concatenate([jnp.where(lane, one, swap(two)), jnp.where(lane, swap(one), two)], axis=1)
            source = source.reshape(256, 128)
            s_rows[h, pl.ds(256 * b, 256)] = source
            dense.append(target * source)
        dense = jnp.concatenate(dense, axis=1)
        along_z = jnp.dot(dense, z_in[...], preferred_element_type=F32).astype(BF16)
        along_y = jnp.dot(y_in[...], along_z, preferred_element_type=F32)
        for h in range(2):
            field[h, pl.ds(256 * b, 256)] = along_y[:, 128 * h : 128 * h + 128]
        return carry

    lax.fori_loop(0, 16, enter, 0)

    def middle(b, carry):
        sides = []
        for h in range(2):
            sides.append(
                jnp.concatenate([field[h, pl.ds(4 * b + k, 64, stride=64)].astype(BF16) for k in range(4)], axis=0)
            )
        waves = jnp.dot(x_in[...], jnp.concatenate(sides, axis=1), preferred_element_type=F32)
        factor = d_ref[pl.ds(4 * b, 4)].reshape(256, 128)
        waves = (waves * jnp.concatenate([factor, factor], axis=1)).astype(BF16)
        back = jnp.dot(x_out[...], waves, preferred_element_type=F32)
        for h in range(2):
            for k in range(4):
                field[h, pl.ds(4 * b + k, 64, stride=64)] = back[64 * k : 64 * k + 64, 128 * h : 128 * h + 128]
        return carry

    lax.fori_loop(0, 16, middle, 0)

    for j in range(4):
        owner = lax.rem(x + j, 4)

        def leave(z, carry):
            rows = pl.ds(256 * (4 * z + owner), 256)
            waves = jnp.concatenate([field[0, rows].astype(BF16), field[1, rows].astype(BF16)], axis=1)
            along_y = jnp.dot(y_out[...], waves, preferred_element_type=F32).astype(BF16)
            along_z = jnp.dot(along_y, z_out[...], preferred_element_type=F32)
            terms = along_z[:, :128] * s_rows[0, rows].astype(F32) + along_z[:, 128:] * s_rows[1, rows].astype(F32)
            terms = terms.reshape(4, 64, 128)
            terms = terms + swap(terms)
            outs[j][z] = jnp.where(lane, terms[:, :32], terms[:, 32:]).astype(outs[j].dtype)
            return carry

        lax.fori_loop(0, 4, leave, 0)


def pair_sums(targets, sources, factor):
    vmem, anywhere = pl.BlockSpec(memory_space=pltpu.VMEM), pl.BlockSpec(memory_space=pl.ANY)
    return pl.pallas_call(
        pair_kernel,
        out_shape=[jax.ShapeDtypeStruct((4, 4, 32, 128), F32 if j == 0 else BF16) for j in range(4)],
        in_specs=[anywhere] * 12 + [vmem] * 7,
        out_specs=[vmem] * 4,
        scratch_shapes=[
            pltpu.VMEM((16, 4, 32, 128), BF16),
            pltpu.VMEM((4, 16, 4, 32, 128), BF16),
            pltpu.VMEM((2, G * G, 128), BF16),
            pltpu.VMEM((2, G * G, 128), F32),
            pltpu.SemaphoreType.DMA((16,)),
            pltpu.SemaphoreType.DMA((64,)),
        ],
        compiler_params=pltpu.CompilerParams(vmem_limit_bytes=40 << 20),
    )(*targets, *sources, factor, *basis_blocks())


def turn(n, by):
    return [(i, (i + by) % n) for i in range(n)]


def shards(targets, sources, exponents, coefficients):
    zl = lax.axis_index("zl")
    packed = targets.reshape(4, 4, 32, 128)
    pick = lambda a, k: lax.dynamic_index_in_dim(a, (zl + k) % 4, 0, keepdims=False)
    mine = sources.reshape(4, 32, 128)
    from_z = [mine] + [lax.ppermute(mine, ("zh", "zl"), turn(8, j)) for j in range(1, 8)]
    from_zl = [pick(packed, 0)] + [lax.ppermute(pick(packed, k), "zl", turn(4, k)) for k in range(1, 4)]
    factor = spectrum(exponents, coefficients)
    source_block = jnp.stack(from_z)
    by_y = [source_block] + [lax.ppermute(source_block, "y", turn(4, i)) for i in range(1, 4)]
    target_block = jnp.stack(from_zl)
    by_x = [target_block] + [lax.ppermute(target_block, "x", turn(4, j)) for j in range(1, 4)]
    by_core = []
    for block in by_y:
        by_core += [block, lax.ppermute(block, "c", turn(2, 1))]
    parts = pair_sums(by_x, by_core, factor)
    summed = parts[0]
    for j in range(1, 4):
        summed = summed + lax.ppermute(parts[j], "x", turn(4, j)).astype(F32)
    rows = [pick(summed, 0)] + [lax.ppermute(pick(summed, k), "zl", turn(4, k)) for k in range(1, 4)]
    rows = jnp.stack(rows[:1] + rows[:0:-1])
    rows = jnp.concatenate([rows, rows])
    rows = lax.dynamic_slice_in_dim(rows, (4 - zl) % 4, 4, 0)
    return -rows.reshape(4, 4, G * G).transpose(1, 0, 2)


def solution(mesh):
    torus = Mesh(mesh.devices.reshape(2, 4, 2, 4, 4), ("zh", "y", "c", "zl", "x"))
    tgt, src = ("zh", "y", "c"), ("zl", "x")
    return jax.shard_map(
        shards,
        mesh=torus,
        in_specs=(P(tgt, src, None), P(src, tgt, None), P(), P()),
        out_specs=P(src, tgt, None),
        check_vma=False,
    )
```

```python
import functools

import jax
import jax.numpy as jnp
import numpy as np
from jax import lax
from jax.experimental import pallas as pl
from jax.experimental.pallas import tpu as pltpu
from jax.sharding import Mesh
from jax.sharding import PartitionSpec as P

G = 64
GAUSS = 8
BF16, F32 = jnp.bfloat16, jnp.float32

SCALE = {0: 1.0, 1: 1.869537353515625, 2: 1.62451171875, 4: 1.13287353515625, 8: 1.8672027587890625, 16: 1.0, 32: 1.0}


def basis():
    n = np.arange(G)
    waves = [(k, np.cos) for k in range(G // 2 + 1)] + [(k, np.sin) for k in range(1, G // 2)]
    rows = np.stack([SCALE[k & -k] * wave(2 * np.pi * k * n / G) for k, wave in waves])
    rows[np.abs(rows) < 1e-12] = 0
    return rows, np.array([k for k, _ in waves])


def basis_blocks():
    rows, _ = basis()
    parity = np.array([2 * r + h for h in range(2) for r in range(32)])
    four = np.eye(4)
    z_in = np.kron(four, rows.T)
    y_in = np.einsum("ky,ab->kbay", rows[:, parity], four).reshape(256, 256)
    x_in = np.einsum("kbx,ij->ikbjx", rows.reshape(G, 16, 4), four).reshape(256, 256)
    return [jnp.asarray(m, BF16) for m in (z_in, y_in, x_in, x_in.T, y_in.T, z_in.T)]


def spectrum(exponents, coefficients):
    rows, freq = basis()
    n = np.arange(G)
    distance = np.minimum(n, G - n).astype(np.float32)
    table = jnp.exp(-exponents[:, None] * (distance * distance)[None])
    weighted = (coefficients[:, None] * table).astype(BF16).astype(F32)
    table = table.astype(BF16).astype(F32)
    waves = jnp.asarray(np.cos(2 * np.pi * np.outer(n, freq) / G) / (rows * rows).sum(1)[None], F32)
    plain = jnp.dot(table, waves, precision=lax.Precision.HIGHEST)
    scaled = jnp.dot(weighted, waves, precision=lax.Precision.HIGHEST)
    scaled = jnp.concatenate([scaled, scaled], axis=1)
    total = 0
    for g in range(GAUSS):
        total = total + (plain[g][:, None] * plain[g][None, :])[:, :, None] * scaled[g][None, None, :]
    return total


def pair_kernel(*refs):
    t_in, s_in, d_ref = refs[:4], refs[4:12], refs[12]
    z_in, y_in, x_in, x_out, y_out, z_out = refs[13:19]
    outs = refs[19:23]
    t_all, s_rows, field = refs[23:]
    zh, y, c, zl, x = (lax.axis_index(a) for a in ("zh", "y", "c", "zl", "x"))
    lane = lax.broadcasted_iota(jnp.int32, (4, 32, 128), 2) < 64

    def swap(a):
        return pltpu.roll(a, 64, 2)

    def dot(a, b):
        return jnp.dot(a, b, preferred_element_type=F32)

    for j in range(4):
        for k in range(4):
            t_all[lax.rem(zl - k + 4, 4) * 4 + lax.rem(x - j + 4, 4)] = t_in[j][k]

    for i in range(4):
        for e in range(2):
            for m in range(2):
                high = (zh + m) % 2
                b = high * 8 + lax.rem(y - i + 4, 4) * 2 + (c if e == 0 else 1 - c)
                target = t_all[b]
                turned = swap(target)
                target = jnp.concatenate([jnp.where(lane, target, turned), jnp.where(lane, turned, target)], axis=1)
                target = target.reshape(256, 128)
                own = [s_in[2 * i + e][p + 4 * lax.rem(m + (zl < p).astype(jnp.int32), 2)] for p in range(4)]
                dense = []
                for h in range(2):
                    one, two = own[2 * h], own[2 * h + 1]
                    source = jnp.concatenate([jnp.where(lane, one, swap(two)), jnp.where(lane, swap(one), two)], axis=1)
                    source = source.reshape(256, 128)
                    s_rows[b, :, 128 * h : 128 * h + 128] = source
                    dense.append(target * source)
                along_z = dot(jnp.concatenate(dense, axis=1), z_in[...]).astype(BF16)
                field[b] = dot(y_in[...], along_z).astype(BF16)

    for k in range(16):
        rows = slice(16 * k, 16 * k + 16)
        waves = dot(x_in[...], field[:, rows, :].reshape(256, 256))
        factor = d_ref[4 * k : 4 * k + 4].reshape(256, 128)
        waves = (waves * jnp.concatenate([factor, factor], axis=1)).astype(BF16)
        field[:, rows, :] = dot(x_out[...], waves).astype(BF16).reshape(16, 16, 256)

    for j in range(4):
        for z in range(4):
            b = 4 * z + lax.rem(x + j, 4)
            along_y = dot(y_out[...], field[b]).astype(BF16)
            terms = dot(along_y, z_out[...]) * s_rows[b].astype(F32)
            terms = (terms[:, :128] + terms[:, 128:]).reshape(4, G, 128)
            terms = terms + swap(terms)
            outs[j][z] = jnp.where(lane, terms[:, :32], terms[:, 32:]).astype(outs[j].dtype)


def pair_sums(targets, sources, factor):
    vmem = pl.BlockSpec(memory_space=pltpu.VMEM)
    return pl.pallas_call(
        pair_kernel,
        out_shape=[jax.ShapeDtypeStruct((4, 4, 32, 128), F32 if j == 0 else BF16) for j in range(4)],
        in_specs=[vmem] * 19,
        out_specs=[vmem] * 4,
        scratch_shapes=[
            pltpu.VMEM((16, 4, 32, 128), BF16),
            pltpu.VMEM((16, 256, 256), BF16),
            pltpu.VMEM((16, 256, 256), BF16),
        ],
        compiler_params=pltpu.CompilerParams(vmem_limit_bytes=24 << 20),
    )(*targets, *sources, factor, *basis_blocks())


def turn(n, by):
    return [(i, (i + by) % n) for i in range(n)]


def shards(targets, sources, exponents, coefficients):
    zl = lax.axis_index("zl")
    packed = targets.reshape(4, 4, 32, 128)
    pick = lambda a, k: lax.dynamic_index_in_dim(a, (zl + k) % 4, 0, keepdims=False)
    mine = sources.reshape(4, 32, 128)
    from_z = [mine] + [lax.ppermute(mine, ("zh", "zl"), turn(8, j)) for j in range(1, 8)]
    from_zl = [pick(packed, 0)] + [lax.ppermute(pick(packed, k), "zl", turn(4, k)) for k in range(1, 4)]
    factor = spectrum(exponents, coefficients)
    source_block = jnp.stack(from_z)
    by_y = [source_block] + [lax.ppermute(source_block, "y", turn(4, i)) for i in range(1, 4)]
    target_block = jnp.stack(from_zl)
    by_x = [target_block] + [lax.ppermute(target_block, "x", turn(4, j)) for j in range(1, 4)]
    by_core = []
    for block in by_y:
        by_core += [block, lax.ppermute(block, "c", turn(2, 1))]
    parts = pair_sums(by_x, by_core, factor)
    summed = parts[0]
    for j in range(1, 4):
        summed = summed + lax.ppermute(parts[j], "x", turn(4, j)).astype(F32)
    rows = [pick(summed, 0)] + [lax.ppermute(pick(summed, k), "zl", turn(4, k)) for k in range(1, 4)]
    rows = jnp.stack(rows[:1] + rows[:0:-1])
    rows = jnp.concatenate([rows, rows])
    rows = lax.dynamic_slice_in_dim(rows, (4 - zl) % 4, 4, 0)
    return -rows.reshape(4, 4, G * G).transpose(1, 0, 2)


def solution(mesh):
    torus = Mesh(mesh.devices.reshape(2, 4, 2, 4, 4), ("zh", "y", "c", "zl", "x"))
    tgt, src = ("zh", "y", "c"), ("zl", "x")
    return jax.shard_map(
        shards,
        mesh=torus,
        in_specs=(P(tgt, src, None), P(src, tgt, None), P(), P()),
        out_specs=P(src, tgt, None),
        check_vma=False,
    )
```

```python
import jax
import jax.numpy as jnp
import numpy as np
from jax import lax
from jax.experimental import pallas as pl
from jax.experimental.pallas import tpu as pltpu
from jax.sharding import Mesh
from jax.sharding import PartitionSpec as P


G = 64
GAUSS = 8
BF16, F32 = jnp.bfloat16, jnp.float32

SCALE = {0: 1.0, 1: 1.869537353515625, 2: 1.62451171875, 4: 1.13287353515625, 8: 1.8672027587890625, 16: 1.0, 32: 1.0}


def basis():
    n = np.arange(G)
    waves = [(k, np.cos) for k in range(G // 2 + 1)] + [(k, np.sin) for k in range(1, G // 2)]
    rows = np.stack([SCALE[k & -k] * wave(2 * np.pi * k * n / G) for k, wave in waves])
    rows[np.abs(rows) < 1e-12] = 0
    return rows, np.array([k for k, _ in waves])


def basis_blocks():
    rows, _ = basis()
    parity = np.array([2 * r + h for h in range(2) for r in range(32)])
    four = np.eye(4)
    z_in = np.kron(four, rows.T)
    y_in = np.einsum("ky,ab->kbay", rows[:, parity], four).reshape(256, 256)
    x_in = np.einsum("kbx,ij->ikbjx", rows.reshape(G, 16, 4), four).reshape(256, 256)
    return [jnp.asarray(m, BF16) for m in (z_in, y_in, x_in, x_in.T, y_in.T, z_in.T)]


def spectrum_kernel(exponents, coefficients, waves, waves_turned, out, outer):
    n = lax.broadcasted_iota(jnp.int32, (GAUSS, G), 1)
    distance = jnp.minimum(n, G - n).astype(F32)
    table = jnp.exp(-exponents[...] * (distance * distance))
    weighted = (coefficients[...] * table).astype(BF16).astype(F32)
    table = table.astype(BF16).astype(F32)
    scaled = jnp.dot(weighted, waves[...], precision=lax.Precision.HIGHEST, preferred_element_type=F32)
    plain = lax.dot_general(
        waves_turned[...], table, (((1,), (1,)), ((), ())), precision=lax.Precision.HIGHEST, preferred_element_type=F32
    )
    for g in range(GAUSS):
        outer[g] = plain[:, g : g + 1] * scaled[g : g + 1]
    for k in range(G):
        total = plain[k : k + 1, 0:1] * outer[0]
        for g in range(1, GAUSS):
            total = total + plain[k : k + 1, g : g + 1] * outer[g]
        out[k] = total


def spectrum(exponents, coefficients):
    rows, freq = basis()
    waves = np.cos(2 * np.pi * np.outer(np.arange(G), freq) / G) / (rows * rows).sum(1)[None]
    return pl.pallas_call(
        spectrum_kernel,
        out_shape=jax.ShapeDtypeStruct((G, G, 128), F32),
        scratch_shapes=[pltpu.VMEM((GAUSS, G, 128), F32)],
        cost_estimate=pl.CostEstimate(flops=8 << 20, bytes_accessed=3 << 20, transcendentals=512),
    )(
        exponents.reshape(GAUSS, 1),
        coefficients.reshape(GAUSS, 1),
        jnp.asarray(np.concatenate([waves, waves], axis=1), F32),
        jnp.asarray(waves.T, F32),
    )


def pair_kernel(*refs):
    t_in, s_in, d_ref = refs[:4], refs[4:6], refs[6]
    z_in, y_in, x_in, x_out, y_out, z_out = refs[7:13]
    out = refs[13]
    t_all, s_rows, field = refs[14:]
    zh, c, zl, x = (lax.axis_index(a) for a in ("zh", "c", "zl", "x"))
    lane = lax.broadcasted_iota(jnp.int32, (4, 32, 128), 2) < 64

    def swap(a):
        return pltpu.roll(a, 64, 2)

    def dot(a, b):
        return jnp.dot(a, b, preferred_element_type=F32)

    for k in range(4):
        for j in range(4):
            t_all[lax.bitwise_xor(zl, k) * 4 + lax.rem(x - j + 4, 4)] = t_in[k][j]

    for e in range(2):
        for y in range(4):
            for m in range(2):
                b = lax.rem(zh + m, 2) * 8 + y * 2 + lax.rem(c + e, 2)
                target = t_all[b]
                turned = swap(target)
                target = jnp.concatenate([jnp.where(lane, target, turned), jnp.where(lane, turned, target)], axis=1)
                target = target.reshape(256, 128)
                dense = []
                for h in range(2):
                    one, two = s_in[e][8 * h + y, m], s_in[e][8 * h + 4 + y, m]
                    source = jnp.concatenate([jnp.where(lane, one, swap(two)), jnp.where(lane, swap(one), two)], axis=1)
                    source = source.reshape(256, 128)
                    s_rows[b, :, 128 * h : 128 * h + 128] = source
                    dense.append(target * source)
                along_z = dot(jnp.concatenate(dense, axis=1), z_in[...]).astype(BF16)
                field[b] = dot(y_in[...], along_z).astype(BF16)

    for k in range(16):
        rows = slice(16 * k, 16 * k + 16)
        waves = dot(x_in[...], field[:, rows, :].reshape(256, 256))
        factor = d_ref[4 * k : 4 * k + 4].reshape(256, 128)
        waves = (waves * jnp.concatenate([factor, factor], axis=1)).astype(BF16)
        field[:, rows, :] = dot(x_out[...], waves).astype(BF16).reshape(16, 16, 256)

    for b in range(16):
        along_y = dot(y_out[...], field[b]).astype(BF16)
        terms = dot(along_y, z_out[...]) * s_rows[b].astype(F32)
        terms = (terms[:, :128] + terms[:, 128:]).reshape(4, G, 128)
        terms = terms + swap(terms)
        out[b] = jnp.where(lane, terms[:, :32], terms[:, 32:]).astype(out.dtype)


def pair_sums(targets, sources, factor):
    vmem = pl.BlockSpec(memory_space=pltpu.VMEM)
    return pl.pallas_call(
        pair_kernel,
        out_shape=jax.ShapeDtypeStruct((16, 4, 32, 128), BF16),
        in_specs=[vmem] * 13,
        out_specs=vmem,
        scratch_shapes=[
            pltpu.VMEM((16, 4, 32, 128), BF16),
            pltpu.VMEM((16, 256, 256), BF16),
            pltpu.VMEM((16, 256, 256), BF16),
        ],
        compiler_params=pltpu.CompilerParams(vmem_limit_bytes=24 << 20),
    )(*targets, *sources, factor, *basis_blocks())


def turn(n, by):
    return [(i, (i + by) % n) for i in range(n)]


def flip(n, by):
    return [(i, i ^ by) for i in range(n)]


def exchange(targets, sources, exponents, coefficients):
    x = lax.axis_index("x")
    mine = sources.reshape(4, 32, 128)
    other = lax.ppermute(mine, "zh", turn(2, 1))
    packed = targets.reshape(4, 4, 32, 128)
    pick = lambda j: lax.dynamic_index_in_dim(packed, (x + j) % 4, 0, keepdims=False)
    target_block = jnp.stack([pick(0)] + [lax.ppermute(pick(j), "x", turn(4, j)) for j in range(1, 4)])
    by_z = [target_block] + [lax.ppermute(target_block, "zl", flip(4, k)) for k in range(1, 4)]
    factor = spectrum(exponents, coefficients)
    source_block = jnp.stack([mine, other])
    source_block = jnp.broadcast_to(source_block, (16, 2, 4, 32, 128))
    own_core = lax.all_to_all(source_block, ("x", "y"), 0, 0, tiled=True)
    other_core = lax.ppermute(own_core, "c", turn(2, 1))
    part = pair_sums(by_z, (own_core, other_core), factor)
    parts = lax.all_to_all(part, ("zl", "x"), 0, 0, tiled=True).reshape(4, 4, 4, G * G)
    return -parts.astype(F32).sum(0).transpose(1, 0, 2)


def solution(mesh):
    torus = Mesh(mesh.devices.reshape(2, 4, 2, 4, 4), ("zh", "y", "c", "zl", "x"))
    tgt, src = ("zh", "y", "c"), ("zl", "x")
    return jax.shard_map(
        exchange,
        mesh=torus,
        in_specs=(P(tgt, src, None), P(src, tgt, None), P(), P()),
        out_specs=P(src, tgt, None),
        check_vma=False,
    )
```

```python
import jax
import jax.numpy as jnp
import numpy as np
from jax import lax
from jax.experimental import pallas as pl
from jax.experimental.pallas import tpu as pltpu
from jax.sharding import Mesh
from jax.sharding import PartitionSpec as P


G = 64
GAUSS = 8
BF16, F32 = jnp.bfloat16, jnp.float32

SCALE = {0: 1.0, 1: 1.869537353515625, 2: 1.62451171875, 4: 1.13287353515625, 8: 1.8672027587890625, 16: 1.0, 32: 1.0}


def basis():
    n = np.arange(G)
    waves = [(k, np.cos) for k in range(G // 2 + 1)] + [(k, np.sin) for k in range(1, G // 2)]
    rows = np.stack([SCALE[k & -k] * wave(2 * np.pi * k * n / G) for k, wave in waves])
    rows[np.abs(rows) < 1e-12] = 0
    return rows, np.array([k for k, _ in waves])


def basis_blocks():
    rows, _ = basis()
    parity = np.array([2 * r + h for h in range(2) for r in range(32)])
    four = np.eye(4)
    z_in = np.kron(four, rows.T)
    y_in = np.einsum("ky,ab->kbay", rows[:, parity], four).reshape(256, 256)
    x_in = np.einsum("kbx,ij->ikbjx", rows.reshape(G, 16, 4), four).reshape(256, 256)
    return [jnp.asarray(m, BF16) for m in (z_in, y_in, x_in, x_in.T, y_in.T, z_in.T)]


def spectrum_kernel(exponents, coefficients, waves, waves_turned, out, outer):
    n = lax.broadcasted_iota(jnp.int32, (GAUSS, G), 1)
    term = lax.broadcasted_iota(jnp.int32, (GAUSS, G), 0)
    distance = jnp.minimum(n, G - n).astype(F32)
    power, weight = jnp.zeros((GAUSS, G), F32), jnp.zeros((GAUSS, G), F32)
    for g in range(GAUSS):
        power = jnp.where(term == g, exponents[g], power)
        weight = jnp.where(term == g, coefficients[g], weight)
    table = jnp.exp(-power * (distance * distance))
    weighted = (weight * table).astype(BF16).astype(F32)
    table = table.astype(BF16).astype(F32)
    scaled = jnp.dot(weighted, waves[...], precision=lax.Precision.HIGHEST, preferred_element_type=F32)
    plain = lax.dot_general(
        waves_turned[...], table, (((1,), (1,)), ((), ())), precision=lax.Precision.HIGHEST, preferred_element_type=F32
    )
    for g in range(GAUSS):
        outer[g] = plain[:40, g : g + 1] * scaled[g : g + 1]
    for k in range(G // 2 + 1):
        total = plain[k : k + 1, 0:1] * outer[0]
        for g in range(1, GAUSS):
            total = total + plain[k : k + 1, g : g + 1] * outer[g]
        for row in (k, G // 2 + k) if 0 < k < G // 2 else (k,):
            out[row, :40] = total
            out[row, 40:] = total[8:32]


def spectrum(exponents, coefficients):
    rows, freq = basis()
    waves = np.cos(2 * np.pi * np.outer(np.arange(G), freq) / G) / (rows * rows).sum(1)[None]
    smem, vmem = pl.BlockSpec(memory_space=pltpu.SMEM), pl.BlockSpec(memory_space=pltpu.VMEM)
    return pl.pallas_call(
        spectrum_kernel,
        out_shape=jax.ShapeDtypeStruct((G, G, 128), F32),
        in_specs=[smem, smem, vmem, vmem],
        out_specs=vmem,
        scratch_shapes=[pltpu.VMEM((GAUSS, 40, 128), F32)],
        cost_estimate=pl.CostEstimate(flops=8 << 20, bytes_accessed=3 << 20, transcendentals=512),
        compiler_params=pltpu.CompilerParams(vmem_limit_bytes=8 << 20),
    )(
        exponents,
        coefficients,
        jnp.asarray(np.concatenate([waves, waves], axis=1), F32),
        jnp.asarray(waves.T, F32),
    )


def pair_kernel(*refs):
    t_in, s_in, d_ref = refs[:4], refs[4:12], refs[12]
    z_in, y_in, x_in, x_out, y_out, z_out = refs[13:19]
    out = refs[19]
    t_all, s_all, s_rows, field = refs[20:]
    zh, y, c, zl, x = (lax.axis_index(a) for a in ("zh", "y", "c", "zl", "x"))
    lane = lax.broadcasted_iota(jnp.int32, (4, 32, 128), 2) < 64

    def swap(a):
        return pltpu.roll(a, 64, 2)

    def dot(a, b):
        return jnp.dot(a, b, preferred_element_type=F32)

    for k in range(4):
        for j in range(4):
            t_all[lax.bitwise_xor(zl, k) * 4 + lax.rem(x - j + 4, 4)] = t_in[k][j]

    for e in range(2):
        core = lax.rem(c + e, 2)
        for l in range(4):
            for i in range(4):
                by_x, by_y = i + core * (l - i), l + core * (i - l)
                for m in range(2):
                    b = lax.rem(zh + m, 2) * 8 + lax.rem(y - by_y + 4, 4) * 2 + core
                    s_all[by_x, b] = s_in[4 * e + l][i, m]

    for b in range(16):
        target = t_all[b]
        turned = swap(target)
        target = jnp.concatenate([jnp.where(lane, target, turned), jnp.where(lane, turned, target)], axis=1)
        target = target.reshape(256, 128)
        dense = []
        for h in range(2):
            one, two = s_all[2 * h, b], s_all[2 * h + 1, b]
            source = jnp.concatenate([jnp.where(lane, one, swap(two)), jnp.where(lane, swap(one), two)], axis=1)
            source = source.reshape(256, 128)
            s_rows[b, :, 128 * h : 128 * h + 128] = source
            dense.append(target * source)
        along_z = dot(jnp.concatenate(dense, axis=1), z_in[...]).astype(BF16)
        field[b] = dot(y_in[...], along_z).astype(BF16)

    for k in range(16):
        rows = slice(16 * k, 16 * k + 16)
        waves = dot(x_in[...], field[:, rows, :].reshape(256, 256))
        factor = d_ref[4 * k : 4 * k + 4].reshape(256, 128)
        waves = (waves * jnp.concatenate([factor, factor], axis=1)).astype(BF16)
        field[:, rows, :] = dot(x_out[...], waves).astype(BF16).reshape(16, 16, 256)

    for b in range(16):
        along_y = dot(y_out[...], field[b]).astype(BF16)
        terms = dot(along_y, z_out[...]) * s_rows[b].astype(F32)
        terms = (terms[:, :128] + terms[:, 128:]).reshape(4, G, 128)
        terms = terms + swap(terms)
        out[b] = jnp.where(lane, terms[:, :32], terms[:, 32:]).astype(out.dtype)


def pair_sums(targets, sources, factor):
    vmem = pl.BlockSpec(memory_space=pltpu.VMEM)
    return pl.pallas_call(
        pair_kernel,
        out_shape=jax.ShapeDtypeStruct((16, 4, 32, 128), BF16),
        in_specs=[vmem] * 19,
        out_specs=vmem,
        scratch_shapes=[
            pltpu.VMEM((16, 4, 32, 128), BF16),
            pltpu.VMEM((4, 16, 4, 32, 128), BF16),
            pltpu.VMEM((16, 256, 256), BF16),
            pltpu.VMEM((16, 256, 256), BF16),
        ],
        compiler_params=pltpu.CompilerParams(vmem_limit_bytes=24 << 20),
    )(*targets, *sources, factor, *basis_blocks())


def turn(n, by):
    return [(i, (i + by) % n) for i in range(n)]


def flip(n, by):
    return [(i, i ^ by) for i in range(n)]


def weave(along_x, along_y):
    place = lambda y, c, x: ((y % 4) * 2 + c) * 4 + x % 4
    pairs = []
    for y in range(4):
        for x in range(4):
            pairs.append((place(y, 0, x), place(y + along_y, 0, x + along_x)))
            pairs.append((place(y, 1, x), place(y + along_x, 1, x + along_y)))
    return pairs


SHIFTS = (1, 3, 2)


def exchange(targets, sources, exponents, coefficients):
    x = lax.axis_index("x")
    mine = sources.reshape(4, 32, 128)
    other = lax.ppermute(mine, "zh", turn(2, 1))
    packed = targets.reshape(4, 4, 32, 128)
    pick = lambda j: lax.dynamic_index_in_dim(packed, (x + j) % 4, 0, keepdims=False)
    rows = {j: lax.ppermute(pick(j), "x", turn(4, j)) for j in SHIFTS}
    target_block = jnp.stack([pick(0)] + [rows[j] for j in range(1, 4)])
    lines = [target_block] + [lax.ppermute(target_block, "zl", flip(4, k)) for k in range(1, 4)]
    factor = spectrum(exponents, coefficients)
    plane = ("y", "c", "x")
    block = jnp.stack([mine, other])
    first = {i: lax.ppermute(block, plane, weave(i, 0)) for i in SHIFTS}
    block = jnp.stack([block] + [first[i] for i in range(1, 4)])
    second = {l: lax.ppermute(block, plane, weave(0, l)) for l in SHIFTS}
    own_core = [block] + [second[l] for l in range(1, 4)]
    other_core = [lax.ppermute(own_core[l], "c", turn(2, 1)) for l in range(4)]
    part = pair_sums(lines, own_core + other_core, factor)
    parts = lax.all_to_all(part, ("zl", "x"), 0, 0, tiled=True).reshape(4, 4, 4, G * G)
    return -parts.astype(F32).sum(0).transpose(1, 0, 2)


def solution(mesh):
    torus = Mesh(mesh.devices.reshape(2, 4, 2, 4, 4), ("zh", "y", "c", "zl", "x"))
    tgt, src = ("zh", "y", "c"), ("zl", "x")
    return jax.shard_map(
        exchange,
        mesh=torus,
        in_specs=(P(tgt, src, None), P(src, tgt, None), P(), P()),
        out_specs=P(src, tgt, None),
        check_vma=False,
    )
```

```python
import jax
import jax.numpy as jnp
import numpy as np
from jax import lax
from jax.experimental import pallas as pl
from jax.experimental.pallas import tpu as pltpu
from jax.sharding import Mesh
from jax.sharding import PartitionSpec as P


G = 64
GAUSS = 8
BF16, F32 = jnp.bfloat16, jnp.float32

SCALE = {0: 1.0, 1: 1.869537353515625, 2: 1.62451171875, 4: 1.13287353515625, 8: 1.8672027587890625, 16: 1.0, 32: 1.0}


def basis():
    n = np.arange(G)
    waves = [(k, np.cos) for k in range(G // 2 + 1)] + [(k, np.sin) for k in range(1, G // 2)]
    rows = np.stack([SCALE[k & -k] * wave(2 * np.pi * k * n / G) for k, wave in waves])
    rows[np.abs(rows) < 1e-12] = 0
    return rows, np.array([k for k, _ in waves])


def basis_blocks():
    rows, _ = basis()
    parity = np.array([2 * r + h for h in range(2) for r in range(32)])
    four = np.eye(4)
    z_in = np.kron(four, rows.T)
    y_in = np.einsum("ky,ab->kbay", rows[:, parity], four).reshape(256, 256)
    x_in = np.einsum("kbx,ij->ikbjx", rows.reshape(G, 16, 4), four).reshape(256, 256)
    return [jnp.asarray(m, BF16) for m in (z_in, y_in, x_in, x_in.T, y_in.T, z_in.T)]


def spectrum_kernel(exponents, coefficients, waves, waves_turned, out, outer):
    n = lax.broadcasted_iota(jnp.int32, (GAUSS, G), 1)
    term = lax.broadcasted_iota(jnp.int32, (GAUSS, G), 0)
    distance = jnp.minimum(n, G - n).astype(F32)
    power, weight = jnp.zeros((GAUSS, G), F32), jnp.zeros((GAUSS, G), F32)
    for g in range(GAUSS):
        power = jnp.where(term == g, exponents[g], power)
        weight = jnp.where(term == g, coefficients[g], weight)
    table = jnp.exp(-power * (distance * distance))
    weighted = (weight * table).astype(BF16).astype(F32)
    table = table.astype(BF16).astype(F32)
    scaled = jnp.dot(weighted, waves[...], precision=lax.Precision.HIGHEST, preferred_element_type=F32)
    plain = lax.dot_general(
        waves_turned[...], table, (((1,), (1,)), ((), ())), precision=lax.Precision.HIGHEST, preferred_element_type=F32
    )
    for g in range(GAUSS):
        outer[g] = plain[:40, g : g + 1] * scaled[g : g + 1]
    for k in range(G // 2 + 1):
        total = plain[k : k + 1, 0:1] * outer[0]
        for g in range(1, GAUSS):
            total = total + plain[k : k + 1, g : g + 1] * outer[g]
        for row in (k, G // 2 + k) if 0 < k < G // 2 else (k,):
            out[row, :40] = total
            out[row, 40:] = total[8:32]


def spectrum(exponents, coefficients):
    rows, freq = basis()
    waves = np.cos(2 * np.pi * np.outer(np.arange(G), freq) / G) / (rows * rows).sum(1)[None]
    smem, vmem = pl.BlockSpec(memory_space=pltpu.SMEM), pl.BlockSpec(memory_space=pltpu.VMEM)
    return pl.pallas_call(
        spectrum_kernel,
        out_shape=jax.ShapeDtypeStruct((G, G, 128), F32),
        in_specs=[smem, smem, vmem, vmem],
        out_specs=vmem,
        scratch_shapes=[pltpu.VMEM((GAUSS, 40, 128), F32)],
        cost_estimate=pl.CostEstimate(flops=8 << 20, bytes_accessed=3 << 20, transcendentals=512),
        compiler_params=pltpu.CompilerParams(vmem_limit_bytes=8 << 20),
    )(
        exponents,
        coefficients,
        jnp.asarray(np.concatenate([waves, waves], axis=1), F32),
        jnp.asarray(waves.T, F32),
    )


def pair_kernel(*refs):
    t_in, s_in, d_ref = refs[:4], refs[4:12], refs[12]
    z_in, y_in, x_in, x_out, y_out, z_out = refs[13:19]
    out = refs[19]
    t_all, s_all, s_rows, field = refs[20:]
    zh, y, c, zl, x = (lax.axis_index(a) for a in ("zh", "y", "c", "zl", "x"))
    lane = lax.broadcasted_iota(jnp.int32, (4, 32, 128), 2) < 64

    def swap(a):
        return pltpu.roll(a, 64, 2)

    def dot(a, b):
        return jnp.dot(a, b, preferred_element_type=F32)

    for k in range(4):
        for j in range(4):
            t_all[lax.bitwise_xor(zl, k) * 4 + lax.rem(x - j + 4, 4)] = t_in[k][j]

    for e in range(2):
        core = lax.rem(c + e, 2)
        for l in range(4):
            for i in range(4):
                by_x, by_y = i + core * (l - i), l + core * (i - l)
                for m in range(2):
                    b = lax.rem(zh + m, 2) * 8 + lax.rem(y - by_y + 4, 4) * 2 + core
                    s_all[by_x, b] = s_in[4 * e + l][i, m]

    for b in range(16):
        target = t_all[b]
        turned = swap(target)
        target = jnp.concatenate([jnp.where(lane, target, turned), jnp.where(lane, turned, target)], axis=1)
        target = target.reshape(256, 128)
        dense = []
        for h in range(2):
            one, two = s_all[2 * h, b], s_all[2 * h + 1, b]
            source = jnp.concatenate([jnp.where(lane, one, swap(two)), jnp.where(lane, swap(one), two)], axis=1)
            source = source.reshape(256, 128)
            s_rows[b, :, 128 * h : 128 * h + 128] = source
            dense.append(target * source)
        along_z = dot(jnp.concatenate(dense, axis=1), z_in[...]).astype(BF16)
        field[b] = dot(y_in[...], along_z).astype(BF16)

    for k in range(16):
        rows = slice(16 * k, 16 * k + 16)
        waves = dot(x_in[...], field[:, rows, :].reshape(256, 256))
        factor = d_ref[4 * k : 4 * k + 4].reshape(256, 128)
        waves = (waves * jnp.concatenate([factor, factor], axis=1)).astype(BF16)
        field[:, rows, :] = dot(x_out[...], waves).astype(BF16).reshape(16, 16, 256)

    for b in range(16):
        along_y = dot(y_out[...], field[b]).astype(BF16)
        terms = dot(along_y, z_out[...]) * s_rows[b].astype(F32)
        terms = (terms[:, :128] + terms[:, 128:]).reshape(4, G, 128)
        terms = terms + swap(terms)
        out[b] = jnp.where(lane, terms[:, :32], terms[:, 32:]).astype(out.dtype)


def pair_sums(targets, sources, factor):
    vmem = pl.BlockSpec(memory_space=pltpu.VMEM)
    return pl.pallas_call(
        pair_kernel,
        out_shape=jax.ShapeDtypeStruct((16, 4, 32, 128), BF16),
        in_specs=[vmem] * 19,
        out_specs=vmem,
        scratch_shapes=[
            pltpu.VMEM((16, 4, 32, 128), BF16),
            pltpu.VMEM((4, 16, 4, 32, 128), BF16),
            pltpu.VMEM((16, 256, 256), BF16),
            pltpu.VMEM((16, 256, 256), BF16),
        ],
        compiler_params=pltpu.CompilerParams(vmem_limit_bytes=24 << 20),
    )(*targets, *sources, factor, *basis_blocks())


def turn(n, by):
    return [(i, (i + by) % n) for i in range(n)]


def flip(n, by):
    return [(i, i ^ by) for i in range(n)]


def weave(along_x, along_y):
    place = lambda y, c, x: ((y % 4) * 2 + c) * 4 + x % 4
    pairs = []
    for y in range(4):
        for x in range(4):
            pairs.append((place(y, 0, x), place(y + along_y, 0, x + along_x)))
            pairs.append((place(y, 1, x), place(y + along_x, 1, x + along_y)))
    return pairs


SHIFTS = (2, 1, 3)


def exchange(targets, sources, exponents, coefficients):
    x = lax.axis_index("x")
    pick = lambda j: lax.dynamic_index_in_dim(targets, (x + j) % 4, 0, keepdims=False)
    rows = {j: lax.ppermute(pick(j), "x", turn(4, j)) for j in SHIFTS}
    mine = sources.reshape(4, 32, 128)
    other = lax.ppermute(mine, "zh", turn(2, 1))
    target_block = jnp.stack([pick(0)] + [rows[j] for j in range(1, 4)]).reshape(4, 4, 32, 128)
    lines = [target_block] + [lax.ppermute(target_block, "zl", flip(4, k)) for k in range(1, 4)]
    factor = spectrum(exponents, coefficients)
    plane = ("y", "c", "x")
    block = jnp.stack([mine, other])
    first = {i: lax.ppermute(block, plane, weave(i, 0)) for i in SHIFTS}
    block = jnp.stack([block] + [first[i] for i in range(1, 4)])
    second = {l: lax.ppermute(block, plane, weave(0, l)) for l in SHIFTS}
    own_core = [block] + [second[l] for l in range(1, 4)]
    other_core = [lax.ppermute(own_core[l], "c", turn(2, 1)) for l in range(4)]
    part = pair_sums(lines, own_core + other_core, factor)
    parts = lax.all_to_all(part, ("zl", "x"), 0, 0, tiled=True).reshape(4, 4, 4, G * G)
    return -parts.astype(F32).sum(0).transpose(1, 0, 2)


def solution(mesh):
    torus = Mesh(mesh.devices.reshape(2, 4, 2, 4, 4), ("zh", "y", "c", "zl", "x"))
    tgt, src = ("zh", "y", "c"), ("zl", "x")
    return jax.shard_map(
        exchange,
        mesh=torus,
        in_specs=(P(tgt, src, None), P(src, tgt, None), P(), P()),
        out_specs=P(src, tgt, None),
        check_vma=False,
    )
```

```python
import jax
import jax.numpy as jnp
import numpy as np
from jax import lax
from jax.experimental import pallas as pl
from jax.experimental.pallas import tpu as pltpu
from jax.sharding import Mesh
from jax.sharding import PartitionSpec as P


G = 64
GAUSS = 8
BF16, F32 = jnp.bfloat16, jnp.float32

SCALE = {0: 1.0, 1: 1.869537353515625, 2: 1.62451171875, 4: 1.13287353515625, 8: 1.8672027587890625, 16: 1.0, 32: 1.0}


def basis():
    n = np.arange(G)
    waves = [(k, np.cos) for k in range(G // 2 + 1)] + [(k, np.sin) for k in range(1, G // 2)]
    rows = np.stack([SCALE[k & -k] * wave(2 * np.pi * k * n / G) for k, wave in waves])
    rows[np.abs(rows) < 1e-12] = 0
    return rows, np.array([k for k, _ in waves])


def basis_blocks():
    rows, _ = basis()
    parity = np.array([2 * r + h for h in range(2) for r in range(32)])
    four = np.eye(4)
    z_in = np.kron(four, rows.T)
    y_in = np.einsum("ky,ab->kbay", rows[:, parity], four).reshape(256, 256)
    x_in = np.einsum("kbx,ij->ikbjx", rows.reshape(G, 16, 4), four).reshape(256, 256)
    return [jnp.asarray(m, BF16) for m in (z_in, y_in, x_in, x_in.T, y_in.T, z_in.T)]


def waves():
    rows, freq = basis()
    table = np.cos(2 * np.pi * np.outer(np.arange(G), freq) / G) / (rows * rows).sum(1)[None]
    return jnp.asarray(np.concatenate([table, table], axis=1), F32)


def spectrum(exponents, coefficients, table, out, outer):
    n = lax.broadcasted_iota(jnp.int32, (GAUSS, G), 1)
    term = lax.broadcasted_iota(jnp.int32, (GAUSS, G), 0)
    distance = jnp.minimum(n, G - n).astype(F32)
    power, weight = jnp.zeros((GAUSS, G), F32), jnp.zeros((GAUSS, G), F32)
    for g in range(GAUSS):
        power = jnp.where(term == g, exponents[g], power)
        weight = jnp.where(term == g, coefficients[g], weight)
    kernel = jnp.exp(-power * (distance * distance))
    weighted = (weight * kernel).astype(BF16).astype(F32)
    kernel = kernel.astype(BF16).astype(F32)
    scaled, plain = jnp.zeros((GAUSS, 128), F32), jnp.zeros((GAUSS, 128), F32)
    for k in range(G):
        row = table[k : k + 1]
        scaled = scaled + weighted[:, k : k + 1] * row
        plain = plain + kernel[:, k : k + 1] * row
    plain = plain.T
    for g in range(GAUSS):
        outer[g] = plain[:40, g : g + 1] * scaled[g : g + 1]
    for k in range(G // 2 + 1):
        total = plain[k : k + 1, 0:1] * outer[0]
        for g in range(1, GAUSS):
            total = total + plain[k : k + 1, g : g + 1] * outer[g]
        for row in (k, G // 2 + k) if 0 < k < G // 2 else (k,):
            out[row, :40] = total
            out[row, 40:] = total[8:32]


def pair_kernel(*refs):
    t_in, s_in = refs[:4], refs[4:12]
    exponents, coefficients, table, z_in, y_in, x_in, x_out, y_out, z_out, out = refs[12:22]
    t_all, s_all, s_rows, field, d_ref, outer = refs[22:]
    zh, y, c, zl, x = (lax.axis_index(a) for a in ("zh", "y", "c", "zl", "x"))
    lane = lax.broadcasted_iota(jnp.int32, (4, 32, 128), 2) < 64

    def swap(a):
        return pltpu.roll(a, 64, 2)

    def dot(a, b):
        return jnp.dot(a, b, preferred_element_type=F32)

    spectrum(exponents, coefficients, table, d_ref, outer)
    for k in range(4):
        for j in range(4):
            t_all[lax.bitwise_xor(zl, k) * 4 + lax.rem(x - j + 4, 4)] = t_in[k][j]

    for e in range(2):
        core = lax.rem(c + e, 2)
        for l in range(4):
            for i in range(4):
                by_x, by_y = i + core * (l - i), l + core * (i - l)
                for m in range(2):
                    b = lax.rem(zh + m, 2) * 8 + lax.rem(y - by_y + 4, 4) * 2 + core
                    s_all[by_x, b] = s_in[4 * e + l][i, m]

    for b in range(16):
        target = t_all[b]
        turned = swap(target)
        target = jnp.concatenate([jnp.where(lane, target, turned), jnp.where(lane, turned, target)], axis=1)
        target = target.reshape(256, 128)
        dense = []
        for h in range(2):
            one, two = s_all[2 * h, b], s_all[2 * h + 1, b]
            source = jnp.concatenate([jnp.where(lane, one, swap(two)), jnp.where(lane, swap(one), two)], axis=1)
            source = source.reshape(256, 128)
            s_rows[b, :, 128 * h : 128 * h + 128] = source
            dense.append(target * source)
        along_z = dot(jnp.concatenate(dense, axis=1), z_in[...]).astype(BF16)
        field[b] = dot(y_in[...], along_z).astype(BF16)

    for k in range(16):
        rows = slice(16 * k, 16 * k + 16)
        waves = dot(x_in[...], field[:, rows, :].reshape(256, 256))
        factor = d_ref[4 * k : 4 * k + 4].reshape(256, 128)
        waves = (waves * jnp.concatenate([factor, factor], axis=1)).astype(BF16)
        field[:, rows, :] = dot(x_out[...], waves).astype(BF16).reshape(16, 16, 256)

    for b in range(16):
        along_y = dot(y_out[...], field[b]).astype(BF16)
        terms = dot(along_y, z_out[...]) * s_rows[b].astype(F32)
        terms = (terms[:, :128] + terms[:, 128:]).reshape(4, G, 128)
        terms = terms + swap(terms)
        out[b] = jnp.where(lane, terms[:, :32], terms[:, 32:]).astype(out.dtype)


def pair_sums(targets, sources, exponents, coefficients):
    vmem, smem = pl.BlockSpec(memory_space=pltpu.VMEM), pl.BlockSpec(memory_space=pltpu.SMEM)
    return pl.pallas_call(
        pair_kernel,
        out_shape=jax.ShapeDtypeStruct((16, 4, 32, 128), BF16),
        in_specs=[vmem] * 12 + [smem] * 2 + [vmem] * 7,
        out_specs=vmem,
        scratch_shapes=[
            pltpu.VMEM((16, 4, 32, 128), BF16),
            pltpu.VMEM((4, 16, 4, 32, 128), BF16),
            pltpu.VMEM((16, 256, 256), BF16),
            pltpu.VMEM((16, 256, 256), BF16),
            pltpu.VMEM((G, G, 128), F32),
            pltpu.VMEM((GAUSS, 40, 128), F32),
        ],
        compiler_params=pltpu.CompilerParams(vmem_limit_bytes=24 << 20),
    )(*targets, *sources, exponents, coefficients, waves(), *basis_blocks())


def turn(n, by):
    return [(i, (i + by) % n) for i in range(n)]


def flip(n, by):
    return [(i, i ^ by) for i in range(n)]


def weave(along_x, along_y):
    place = lambda y, c, x: ((y % 4) * 2 + c) * 4 + x % 4
    pairs = []
    for y in range(4):
        for x in range(4):
            pairs.append((place(y, 0, x), place(y + along_y, 0, x + along_x)))
            pairs.append((place(y, 1, x), place(y + along_x, 1, x + along_y)))
    return pairs


SHIFTS = (2, 1, 3)


def exchange(targets, sources, exponents, coefficients):
    x = lax.axis_index("x")
    mine = sources.reshape(4, 32, 128)
    other = lax.ppermute(mine, "zh", turn(2, 1))
    packed = targets.reshape(4, 4, 32, 128)
    pick = lambda j: lax.dynamic_index_in_dim(packed, (x + j) % 4, 0, keepdims=False)
    rows = {j: lax.ppermute(pick(j), "x", turn(4, j)) for j in SHIFTS}
    target_block = jnp.stack([pick(0)] + [rows[j] for j in range(1, 4)])
    lines = [target_block] + [lax.ppermute(target_block, "zl", flip(4, k)) for k in range(1, 4)]
    plane = ("y", "c", "x")
    block = jnp.stack([mine, other])
    first = {i: lax.ppermute(block, plane, weave(i, 0)) for i in SHIFTS}
    block = jnp.stack([block] + [first[i] for i in range(1, 4)])
    second = {l: lax.ppermute(block, plane, weave(0, l)) for l in SHIFTS}
    own_core = [block] + [second[l] for l in range(1, 4)]
    other_core = [lax.ppermute(own_core[l], "c", turn(2, 1)) for l in range(4)]
    part = pair_sums(lines, own_core + other_core, exponents, coefficients)
    parts = lax.all_to_all(part, ("zl", "x"), 0, 0, tiled=True).reshape(4, 4, 4, G * G)
    return -parts.astype(F32).sum(0).transpose(1, 0, 2)


def solution(mesh):
    torus = Mesh(mesh.devices.reshape(2, 4, 2, 4, 4), ("zh", "y", "c", "zl", "x"))
    tgt, src = ("zh", "y", "c"), ("zl", "x")
    return jax.shard_map(
        exchange,
        mesh=torus,
        in_specs=(P(tgt, src, None), P(src, tgt, None), P(), P()),
        out_specs=P(src, tgt, None),
        check_vma=False,
    )
```

```python
import jax
import jax.numpy as jnp
import numpy as np
from jax import lax
from jax.experimental import pallas as pl
from jax.experimental.pallas import tpu as pltpu
from jax.sharding import Mesh
from jax.sharding import PartitionSpec as P


G = 64
GAUSS = 8
BF16, F32 = jnp.bfloat16, jnp.float32

SCALE = {0: 1.0, 1: 1.869537353515625, 2: 1.62451171875, 4: 1.13287353515625, 8: 1.8672027587890625, 16: 1.0, 32: 1.0}


def basis():
    n = np.arange(G)
    waves = [(k, np.cos) for k in range(G // 2 + 1)] + [(k, np.sin) for k in range(1, G // 2)]
    rows = np.stack([SCALE[k & -k] * wave(2 * np.pi * k * n / G) for k, wave in waves])
    rows[np.abs(rows) < 1e-12] = 0
    return rows, np.array([k for k, _ in waves])


def basis_blocks():
    rows, _ = basis()
    parity = np.array([2 * r + h for h in range(2) for r in range(32)])
    four = np.eye(4)
    z_in = np.kron(four, rows.T)
    y_in = np.einsum("ky,ab->kbay", rows[:, parity], four).reshape(256, 256)
    x_in = np.einsum("kbx,ij->ikbjx", rows.reshape(G, 16, 4), four).reshape(256, 256)
    return [jnp.asarray(m, BF16) for m in (z_in, y_in, x_in, x_in.T, y_in.T, z_in.T)]


def waves():
    rows, freq = basis()
    table = np.cos(2 * np.pi * np.outer(np.arange(G), freq) / G) / (rows * rows).sum(1)[None]
    return jnp.asarray(np.concatenate([table, table], axis=1), F32)


def spectrum(exponents, coefficients, table, out, outer):
    n = lax.broadcasted_iota(jnp.int32, (GAUSS, G), 1)
    term = lax.broadcasted_iota(jnp.int32, (GAUSS, G), 0)
    distance = jnp.minimum(n, G - n).astype(F32)
    power, weight = jnp.zeros((GAUSS, G), F32), jnp.zeros((GAUSS, G), F32)
    for g in range(GAUSS):
        power = jnp.where(term == g, exponents[g], power)
        weight = jnp.where(term == g, coefficients[g], weight)
    kernel = jnp.exp(-power * (distance * distance))
    weighted = (weight * kernel).astype(BF16).astype(F32)
    kernel = kernel.astype(BF16).astype(F32)
    scaled, plain = jnp.zeros((GAUSS, 128), F32), jnp.zeros((GAUSS, 128), F32)
    for k in range(G):
        row = table[k : k + 1]
        scaled = scaled + weighted[:, k : k + 1] * row
        plain = plain + kernel[:, k : k + 1] * row
    plain = plain.T
    for g in range(GAUSS):
        outer[g] = plain[:40, g : g + 1] * scaled[g : g + 1]
    for k in range(G // 2 + 1):
        total = plain[k : k + 1, 0:1] * outer[0]
        for g in range(1, GAUSS):
            total = total + plain[k : k + 1, g : g + 1] * outer[g]
        for row in (k, G // 2 + k) if 0 < k < G // 2 else (k,):
            out[row, :40] = total
            out[row, 40:] = total[8:32]


def pair_kernel(*refs):
    t_in, s_in = refs[:4], refs[4:14]
    exponents, coefficients, table, z_in, y_in, x_in, x_out, y_out, z_out, out = refs[14:24]
    t_all, s_all, s_rows, field, d_ref, outer = refs[24:]
    zh, y, c, zl, x = (lax.axis_index(a) for a in ("zh", "y", "c", "zl", "x"))
    lane = lax.broadcasted_iota(jnp.int32, (4, 32, 128), 2) < 64

    def swap(a):
        return pltpu.roll(a, 64, 2)

    def dot(a, b):
        return jnp.dot(a, b, preferred_element_type=F32)

    spectrum(exponents, coefficients, table, d_ref, outer)
    for k in range(4):
        for j in range(4):
            t_all[lax.bitwise_xor(zl, k) * 4 + lax.rem(x - j + 4, 4)] = t_in[k][j]

    for e in range(2):
        core = lax.rem(c + e, 2)
        for l in range(4):
            for i in range(4):
                by_x, by_y = i + core * (l - i), l + core * (i - l)
                came = s_in[5 * e + (0, 1, 3 + i // 2, 2)[l]]
                for m in range(2):
                    b = lax.rem(zh + m, 2) * 8 + lax.rem(y - by_y + 4, 4) * 2 + core
                    s_all[by_x, b] = came[i % 2 if l == 2 else i, m]

    for b in range(16):
        target = t_all[b]
        turned = swap(target)
        target = jnp.concatenate([jnp.where(lane, target, turned), jnp.where(lane, turned, target)], axis=1)
        target = target.reshape(256, 128)
        dense = []
        for h in range(2):
            one, two = s_all[2 * h, b], s_all[2 * h + 1, b]
            source = jnp.concatenate([jnp.where(lane, one, swap(two)), jnp.where(lane, swap(one), two)], axis=1)
            source = source.reshape(256, 128)
            s_rows[b, :, 128 * h : 128 * h + 128] = source
            dense.append(target * source)
        along_z = dot(jnp.concatenate(dense, axis=1), z_in[...]).astype(BF16)
        field[b] = dot(y_in[...], along_z).astype(BF16)

    for k in range(16):
        rows = slice(16 * k, 16 * k + 16)
        waves = dot(x_in[...], field[:, rows, :].reshape(256, 256))
        factor = d_ref[4 * k : 4 * k + 4].reshape(256, 128)
        waves = (waves * jnp.concatenate([factor, factor], axis=1)).astype(BF16)
        field[:, rows, :] = dot(x_out[...], waves).astype(BF16).reshape(16, 16, 256)

    for b in range(16):
        along_y = dot(y_out[...], field[b]).astype(BF16)
        terms = dot(along_y, z_out[...]) * s_rows[b].astype(F32)
        terms = (terms[:, :128] + terms[:, 128:]).reshape(4, G, 128)
        terms = terms + swap(terms)
        out[b] = jnp.where(lane, terms[:, :32], terms[:, 32:]).astype(out.dtype)


def pair_sums(targets, sources, exponents, coefficients):
    vmem, smem = pl.BlockSpec(memory_space=pltpu.VMEM), pl.BlockSpec(memory_space=pltpu.SMEM)
    return pl.pallas_call(
        pair_kernel,
        out_shape=jax.ShapeDtypeStruct((16, 4, 32, 128), BF16),
        in_specs=[vmem] * 14 + [smem] * 2 + [vmem] * 7,
        out_specs=vmem,
        scratch_shapes=[
            pltpu.VMEM((16, 4, 32, 128), BF16),
            pltpu.VMEM((4, 16, 4, 32, 128), BF16),
            pltpu.VMEM((16, 256, 256), BF16),
            pltpu.VMEM((16, 256, 256), BF16),
            pltpu.VMEM((G, G, 128), F32),
            pltpu.VMEM((GAUSS, 40, 128), F32),
        ],
        compiler_params=pltpu.CompilerParams(vmem_limit_bytes=24 << 20),
    )(*targets, *sources, exponents, coefficients, waves(), *basis_blocks())


def turn(n, by):
    return [(i, (i + by) % n) for i in range(n)]


def flip(n, by):
    return [(i, i ^ by) for i in range(n)]


def weave(along_x, along_y):
    place = lambda y, c, x: ((y % 4) * 2 + c) * 4 + x % 4
    pairs = []
    for y in range(4):
        for x in range(4):
            pairs.append((place(y, 0, x), place(y + along_y, 0, x + along_x)))
            pairs.append((place(y, 1, x), place(y + along_x, 1, x + along_y)))
    return pairs


SHIFTS = (2, 1, 3)


def exchange(targets, sources, exponents, coefficients):
    x = lax.axis_index("x")
    mine = sources.reshape(4, 32, 128)
    other = lax.ppermute(mine, "zh", turn(2, 1))
    packed = targets.reshape(4, 4, 32, 128)
    pick = lambda j: lax.dynamic_index_in_dim(packed, (x + j) % 4, 0, keepdims=False)
    rows = {j: lax.ppermute(pick(j), "x", turn(4, j)) for j in SHIFTS}
    target_block = jnp.stack([pick(0)] + [rows[j] for j in range(1, 4)])
    lines = [target_block] + [lax.ppermute(target_block, "zl", flip(4, k)) for k in range(1, 4)]
    plane = ("y", "c", "x")
    block = jnp.stack([mine, other])
    first = {i: lax.ppermute(block, plane, weave(i, 0)) for i in SHIFTS}
    block = jnp.stack([block] + [first[i] for i in range(1, 4)])
    second = {l: lax.ppermute(block, plane, weave(0, l)) for l in (1, 3)}
    halves = {1: second[1][:2], 3: second[3][2:]}
    third = {l: lax.ppermute(halves[l], plane, weave(0, l)) for l in (1, 3)}
    own_core = [block, second[1], second[3], third[1], third[3]]
    other_core = [lax.ppermute(value, "c", turn(2, 1)) for value in own_core]
    part = pair_sums(lines, own_core + other_core, exponents, coefficients)
    parts = lax.all_to_all(part, ("zl", "x"), 0, 0, tiled=True).reshape(4, 4, 4, G * G)
    return -parts.astype(F32).sum(0).transpose(1, 0, 2)


def solution(mesh):
    torus = Mesh(mesh.devices.reshape(2, 4, 2, 4, 4), ("zh", "y", "c", "zl", "x"))
    tgt, src = ("zh", "y", "c"), ("zl", "x")
    return jax.shard_map(
        exchange,
        mesh=torus,
        in_specs=(P(tgt, src, None), P(src, tgt, None), P(), P()),
        out_specs=P(src, tgt, None),
        check_vma=False,
    )
```

```python
import jax
import jax.numpy as jnp
import numpy as np
from jax import lax
from jax.experimental import pallas as pl
from jax.experimental.pallas import tpu as pltpu
from jax.sharding import Mesh
from jax.sharding import PartitionSpec as P


G = 64
GAUSS = 8
BF16, F32 = jnp.bfloat16, jnp.float32

SCALE = {0: 1.0, 1: 1.869537353515625, 2: 1.62451171875, 4: 1.13287353515625, 8: 1.8672027587890625, 16: 1.0, 32: 1.0}


def basis():
    n = np.arange(G)
    waves = [(k, np.cos) for k in range(G // 2 + 1)] + [(k, np.sin) for k in range(1, G // 2)]
    rows = np.stack([SCALE[k & -k] * wave(2 * np.pi * k * n / G) for k, wave in waves])
    rows[np.abs(rows) < 1e-12] = 0
    return rows, np.array([k for k, _ in waves])


def basis_blocks():
    rows, _ = basis()
    parity = np.array([2 * r + h for h in range(2) for r in range(32)])
    four = np.eye(4)
    z_in = np.kron(four, rows.T)
    y_in = np.einsum("ky,ab->kbay", rows[:, parity], four).reshape(256, 256)
    x_in = np.einsum("kbx,ij->ikbjx", rows.reshape(G, 16, 4), four).reshape(256, 256)
    return [jnp.asarray(m, BF16) for m in (z_in, y_in, x_in, x_in.T, y_in.T, z_in.T)]


def waves():
    rows, freq = basis()
    table = np.cos(2 * np.pi * np.outer(np.arange(G), freq) / G) / (rows * rows).sum(1)[None]
    return jnp.asarray(np.concatenate([table, table], axis=1), F32)


def spectrum(exponents, coefficients, table, out, outer):
    n = lax.broadcasted_iota(jnp.int32, (GAUSS, G), 1)
    term = lax.broadcasted_iota(jnp.int32, (GAUSS, G), 0)
    distance = jnp.minimum(n, G - n).astype(F32)
    power, weight = jnp.zeros((GAUSS, G), F32), jnp.zeros((GAUSS, G), F32)
    for g in range(GAUSS):
        power = jnp.where(term == g, exponents[g], power)
        weight = jnp.where(term == g, coefficients[g], weight)
    kernel = jnp.exp(-power * (distance * distance))
    weighted = (weight * kernel).astype(BF16).astype(F32)
    kernel = kernel.astype(BF16).astype(F32)
    scaled, plain = jnp.zeros((GAUSS, 128), F32), jnp.zeros((GAUSS, 128), F32)
    for k in range(G):
        row = table[k : k + 1]
        scaled = scaled + weighted[:, k : k + 1] * row
        plain = plain + kernel[:, k : k + 1] * row
    plain = plain.T
    for g in range(GAUSS):
        outer[g] = plain[:40, g : g + 1] * scaled[g : g + 1]
    for k in range(G // 2 + 1):
        total = plain[k : k + 1, 0:1] * outer[0]
        for g in range(1, GAUSS):
            total = total + plain[k : k + 1, g : g + 1] * outer[g]
        for row in (k, G // 2 + k) if 0 < k < G // 2 else (k,):
            out[row, :40] = total
            out[row, 40:] = total[8:32]


def pair_kernel(*refs):
    t_in, s_in = refs[:4], refs[4:12]
    exponents, coefficients, table, z_in, y_in, x_in, x_out, y_out, z_out, out = refs[12:22]
    t_all, s_all, s_rows, field, d_ref, outer = refs[22:]
    zh, y, c, zl, x = (lax.axis_index(a) for a in ("zh", "y", "c", "zl", "x"))
    lane = lax.broadcasted_iota(jnp.int32, (4, 32, 128), 2) < 64

    def swap(a):
        return pltpu.roll(a, 64, 2)

    def dot(a, b):
        return jnp.dot(a, b, preferred_element_type=F32)

    spectrum(exponents, coefficients, table, d_ref, outer)
    for k in range(4):
        for j in range(4):
            t_all[lax.bitwise_xor(zl, k) * 4 + lax.rem(x - j + 4, 4)] = t_in[k][j]

    for e in range(2):
        core = lax.rem(c + e, 2)
        for l in range(4):
            for i in range(4):
                by_x, by_y = i + core * (l - i), l + core * (i - l)
                for m in range(2):
                    b = lax.rem(zh + m, 2) * 8 + lax.rem(y - by_y + 4, 4) * 2 + core
                    s_all[by_x, b] = s_in[4 * e + l][i, m]

    for b in range(16):
        target = t_all[b]
        turned = swap(target)
        target = jnp.concatenate([jnp.where(lane, target, turned), jnp.where(lane, turned, target)], axis=1)
        target = target.reshape(256, 128)
        dense = []
        for h in range(2):
            one, two = s_all[2 * h, b], s_all[2 * h + 1, b]
            source = jnp.concatenate([jnp.where(lane, one, swap(two)), jnp.where(lane, swap(one), two)], axis=1)
            source = source.reshape(256, 128)
            s_rows[b, :, 128 * h : 128 * h + 128] = source
            dense.append(target * source)
        along_z = dot(jnp.concatenate(dense, axis=1), z_in[...]).astype(BF16)
        field[b] = dot(y_in[...], along_z).astype(BF16)

    for k in range(16):
        rows = slice(16 * k, 16 * k + 16)
        waves = dot(x_in[...], field[:, rows, :].reshape(256, 256))
        factor = d_ref[4 * k : 4 * k + 4].reshape(256, 128)
        waves = (waves * jnp.concatenate([factor, factor], axis=1)).astype(BF16)
        field[:, rows, :] = dot(x_out[...], waves).astype(BF16).reshape(16, 16, 256)

    for b in range(16):
        along_y = dot(y_out[...], field[b]).astype(BF16)
        terms = dot(along_y, z_out[...]) * s_rows[b].astype(F32)
        terms = (terms[:, :128] + terms[:, 128:]).reshape(4, G, 128)
        terms = terms + swap(terms)
        out[b] = jnp.where(lane, terms[:, :32], terms[:, 32:]).astype(out.dtype)


def pair_sums(targets, sources, exponents, coefficients):
    vmem, smem = pl.BlockSpec(memory_space=pltpu.VMEM), pl.BlockSpec(memory_space=pltpu.SMEM)
    return pl.pallas_call(
        pair_kernel,
        out_shape=jax.ShapeDtypeStruct((16, 4, 32, 128), BF16),
        in_specs=[vmem] * 12 + [smem] * 2 + [vmem] * 7,
        out_specs=vmem,
        scratch_shapes=[
            pltpu.VMEM((16, 4, 32, 128), BF16),
            pltpu.VMEM((4, 16, 4, 32, 128), BF16),
            pltpu.VMEM((16, 256, 256), BF16),
            pltpu.VMEM((16, 256, 256), BF16),
            pltpu.VMEM((G, G, 128), F32),
            pltpu.VMEM((GAUSS, 40, 128), F32),
        ],
        compiler_params=pltpu.CompilerParams(vmem_limit_bytes=24 << 20),
    )(*targets, *sources, exponents, coefficients, waves(), *basis_blocks())


def gather_kernel(parts, out, rows):
    for t in range(4):
        total = parts[t].astype(F32)
        for q in range(1, 4):
            total = total + parts[4 * q + t].astype(F32)
        rows[128 * t : 128 * t + 128] = -total.reshape(128, 128)
    for p in range(4):
        for r in range(32):
            out[p, :, 128 * r : 128 * r + 128] = rows[pl.ds(32 * p + r, 4, stride=128)]


def gathered(parts):
    vmem = pl.BlockSpec(memory_space=pltpu.VMEM)
    return pl.pallas_call(
        gather_kernel,
        out_shape=jax.ShapeDtypeStruct((4, 4, G * G), F32),
        in_specs=[vmem],
        out_specs=vmem,
        scratch_shapes=[pltpu.VMEM((512, 128), F32)],
        compiler_params=pltpu.CompilerParams(vmem_limit_bytes=8 << 20),
    )(parts)


def turn(n, by):
    return [(i, (i + by) % n) for i in range(n)]


def flip(n, by):
    return [(i, i ^ by) for i in range(n)]


def weave(along_x, along_y):
    place = lambda y, c, x: ((y % 4) * 2 + c) * 4 + x % 4
    pairs = []
    for y in range(4):
        for x in range(4):
            pairs.append((place(y, 0, x), place(y + along_y, 0, x + along_x)))
            pairs.append((place(y, 1, x), place(y + along_x, 1, x + along_y)))
    return pairs


SHIFTS = (2, 1, 3)


def exchange(targets, sources, exponents, coefficients):
    x = lax.axis_index("x")
    mine = sources.reshape(4, 32, 128)
    other = lax.ppermute(mine, "zh", turn(2, 1))
    packed = targets.reshape(4, 4, 32, 128)
    pick = lambda j: lax.dynamic_index_in_dim(packed, (x + j) % 4, 0, keepdims=False)
    rows = {j: lax.ppermute(pick(j), "x", turn(4, j)) for j in SHIFTS}
    target_block = jnp.stack([pick(0)] + [rows[j] for j in range(1, 4)])
    lines = [target_block] + [lax.ppermute(target_block, "zl", flip(4, k)) for k in range(1, 4)]
    plane = ("y", "c", "x")
    block = jnp.stack([mine, other])
    first = {i: lax.ppermute(block, plane, weave(i, 0)) for i in SHIFTS}
    block = jnp.stack([block] + [first[i] for i in range(1, 4)])
    second = {l: lax.ppermute(block, plane, weave(0, l)) for l in SHIFTS}
    own_core = [block] + [second[l] for l in range(1, 4)]
    other_core = [lax.ppermute(own_core[l], "c", turn(2, 1)) for l in range(4)]
    part = pair_sums(lines, own_core + other_core, exponents, coefficients)
    parts = lax.all_to_all(part, ("zl", "x"), 0, 0, tiled=True)
    return gathered(parts)


def solution(mesh):
    torus = Mesh(mesh.devices.reshape(2, 4, 2, 4, 4), ("zh", "y", "c", "zl", "x"))
    tgt, src = ("zh", "y", "c"), ("zl", "x")
    return jax.shard_map(
        exchange,
        mesh=torus,
        in_specs=(P(tgt, src, None), P(src, tgt, None), P(), P()),
        out_specs=P(src, tgt, None),
        check_vma=False,
    )
```

```python
import jax
import jax.numpy as jnp
import numpy as np
from jax import lax
from jax.experimental import pallas as pl
from jax.experimental.pallas import tpu as pltpu
from jax.sharding import Mesh
from jax.sharding import PartitionSpec as P


G = 64
GAUSS = 8
BF16, F32 = jnp.bfloat16, jnp.float32

SCALE = {0: 1.0, 1: 1.869537353515625, 2: 1.62451171875, 4: 1.13287353515625, 8: 1.8672027587890625, 16: 1.0, 32: 1.0}


def basis():
    n = np.arange(G)
    waves = [(k, np.cos) for k in range(G // 2 + 1)] + [(k, np.sin) for k in range(1, G // 2)]
    rows = np.stack([SCALE[k & -k] * wave(2 * np.pi * k * n / G) for k, wave in waves])
    rows[np.abs(rows) < 1e-12] = 0
    return rows, np.array([k for k, _ in waves])


def basis_blocks():
    rows, _ = basis()
    parity = np.array([2 * r + h for h in range(2) for r in range(32)])
    four = np.eye(4)
    z_in = np.kron(four, rows.T)
    y_in = np.einsum("ky,ab->kbay", rows[:, parity], four).reshape(256, 256)
    x_in = np.einsum("kbx,ij->ikbjx", rows.reshape(G, 16, 4), four).reshape(256, 256)
    twice = lambda m, axis: np.concatenate([m, m], axis=axis)
    return [jnp.asarray(m, BF16) for m in (z_in, twice(y_in, 1), x_in, twice(x_in.T, 1), y_in.T, twice(z_in.T, 0))]


def waves():
    rows, freq = basis()
    table = np.cos(2 * np.pi * np.outer(np.arange(G), freq) / G) / (rows * rows).sum(1)[None]
    return jnp.asarray(np.concatenate([table, table], axis=1), F32)


def spectrum(exponents, coefficients, table, out, outer):
    n = lax.broadcasted_iota(jnp.int32, (GAUSS, G), 1)
    term = lax.broadcasted_iota(jnp.int32, (GAUSS, G), 0)
    distance = jnp.minimum(n, G - n).astype(F32)
    power, weight = jnp.zeros((GAUSS, G), F32), jnp.zeros((GAUSS, G), F32)
    for g in range(GAUSS):
        power = jnp.where(term == g, exponents[g], power)
        weight = jnp.where(term == g, coefficients[g], weight)
    kernel = jnp.exp(-power * (distance * distance))
    weighted = (weight * kernel).astype(BF16).astype(F32)
    kernel = kernel.astype(BF16).astype(F32)
    scaled, plain = jnp.zeros((GAUSS, 128), F32), jnp.zeros((GAUSS, 128), F32)
    for k in range(G):
        row = table[k : k + 1]
        scaled = scaled + weighted[:, k : k + 1] * row
        plain = plain + kernel[:, k : k + 1] * row
    plain = plain.T
    for g in range(GAUSS):
        outer[g] = plain[:40, g : g + 1] * scaled[g : g + 1]
    for k in range(G // 2 + 1):
        total = plain[k : k + 1, 0:1] * outer[0]
        for g in range(1, GAUSS):
            total = total + plain[k : k + 1, g : g + 1] * outer[g]
        for row in (k, G // 2 + k) if 0 < k < G // 2 else (k,):
            out[row, :40] = total
            out[row, 40:] = total[8:32]


def pair_kernel(*refs):
    t_in, s_in = refs[:4], refs[4:12]
    exponents, coefficients, table, z_in, y_in, x_in, x_out, y_out, z_out, out = refs[12:22]
    t_all, s_all, s_rows, field, d_ref, outer = refs[22:]
    zh, y, c, zl, x = (lax.axis_index(a) for a in ("zh", "y", "c", "zl", "x"))
    lane = lax.broadcasted_iota(jnp.int32, (4, 32, 128), 2) < 64

    def swap(a):
        return pltpu.roll(a, 64, 2)

    def by_fours(step):
        def four(group, carry):
            for n in range(4):
                step(4 * group + n)
            return carry

        lax.fori_loop(0, 4, four, 0)

    def parts(a, axis):
        high = a.astype(BF16)
        return jnp.concatenate([high, (a - high.astype(F32)).astype(BF16)], axis=axis)

    def dot(a, b):
        return jnp.dot(a, b, preferred_element_type=F32)

    spectrum(exponents, coefficients, table, d_ref, outer)
    for k in range(4):
        for j in range(4):
            t_all[lax.bitwise_xor(zl, k) * 4 + lax.rem(x - j + 4, 4)] = t_in[k][j]

    for e in range(2):
        core = lax.rem(c + e, 2)
        for l in range(4):
            for i in range(4):
                by_x, by_y = i + core * (l - i), l + core * (i - l)
                for m in range(2):
                    b = lax.rem(zh + m, 2) * 8 + lax.rem(y - by_y + 4, 4) * 2 + core
                    s_all[by_x, b] = s_in[4 * e + l][i, m]

    def enter(b):
        target = t_all[b]
        turned = swap(target)
        target = jnp.concatenate([jnp.where(lane, target, turned), jnp.where(lane, turned, target)], axis=1)
        target = target.reshape(256, 128)
        dense = []
        for h in range(2):
            one, two = s_all[2 * h, b], s_all[2 * h + 1, b]
            source = jnp.concatenate([jnp.where(lane, one, swap(two)), jnp.where(lane, swap(one), two)], axis=1)
            source = source.reshape(256, 128)
            s_rows[b, :, 128 * h : 128 * h + 128] = source
            dense.append(target * source)
        along_z = dot(jnp.concatenate(dense, axis=1), z_in[...])
        field[b] = dot(y_in[...], parts(along_z, 0)).astype(BF16)

    by_fours(enter)

    for k in range(16):
        rows = slice(16 * k, 16 * k + 16)
        waves = dot(x_in[...], field[:, rows, :].reshape(256, 256))
        factor = d_ref[4 * k : 4 * k + 4].reshape(256, 128)
        waves = parts(waves * jnp.concatenate([factor, factor], axis=1), 0)
        field[:, rows, :] = dot(x_out[...], waves).astype(BF16).reshape(16, 16, 256)

    def leave(b):
        along_y = parts(dot(y_out[...], field[b]), 1)
        terms = dot(along_y, z_out[...]) * s_rows[b].astype(F32)
        terms = (terms[:, :128] + terms[:, 128:]).reshape(4, G, 128)
        terms = terms + swap(terms)
        out[b] = jnp.where(lane, terms[:, :32], terms[:, 32:]).astype(out.dtype)

    by_fours(leave)


def pair_sums(targets, sources, exponents, coefficients):
    vmem, smem = pl.BlockSpec(memory_space=pltpu.VMEM), pl.BlockSpec(memory_space=pltpu.SMEM)
    return pl.pallas_call(
        pair_kernel,
        out_shape=jax.ShapeDtypeStruct((16, 4, 32, 128), BF16),
        in_specs=[vmem] * 12 + [smem] * 2 + [vmem] * 7,
        out_specs=vmem,
        scratch_shapes=[
            pltpu.VMEM((16, 4, 32, 128), BF16),
            pltpu.VMEM((4, 16, 4, 32, 128), BF16),
            pltpu.VMEM((16, 256, 256), BF16),
            pltpu.VMEM((16, 256, 256), BF16),
            pltpu.VMEM((G, G, 128), F32),
            pltpu.VMEM((GAUSS, 40, 128), F32),
        ],
        compiler_params=pltpu.CompilerParams(vmem_limit_bytes=24 << 20),
    )(*targets, *sources, exponents, coefficients, waves(), *basis_blocks())


def gather_kernel(parts, out, rows):
    for t in range(4):
        total = parts[t].astype(F32)
        for q in range(1, 4):
            total = total + parts[4 * q + t].astype(F32)
        rows[128 * t : 128 * t + 128] = -total.reshape(128, 128)
    for p in range(4):
        for r in range(32):
            out[p, :, 128 * r : 128 * r + 128] = rows[pl.ds(32 * p + r, 4, stride=128)]


def gathered(parts):
    vmem = pl.BlockSpec(memory_space=pltpu.VMEM)
    return pl.pallas_call(
        gather_kernel,
        out_shape=jax.ShapeDtypeStruct((4, 4, G * G), F32),
        in_specs=[vmem],
        out_specs=vmem,
        scratch_shapes=[pltpu.VMEM((512, 128), F32)],
        compiler_params=pltpu.CompilerParams(vmem_limit_bytes=8 << 20),
    )(parts)


def turn(n, by):
    return [(i, (i + by) % n) for i in range(n)]


def flip(n, by):
    return [(i, i ^ by) for i in range(n)]


def weave(along_x, along_y):
    place = lambda y, c, x: ((y % 4) * 2 + c) * 4 + x % 4
    pairs = []
    for y in range(4):
        for x in range(4):
            pairs.append((place(y, 0, x), place(y + along_y, 0, x + along_x)))
            pairs.append((place(y, 1, x), place(y + along_x, 1, x + along_y)))
    return pairs


SHIFTS = (2, 1, 3)


def exchange(targets, sources, exponents, coefficients):
    x = lax.axis_index("x")
    mine = sources.reshape(4, 32, 128)
    other = lax.ppermute(mine, "zh", turn(2, 1))
    packed = targets.reshape(4, 4, 32, 128)
    pick = lambda j: lax.dynamic_index_in_dim(packed, (x + j) % 4, 0, keepdims=False)
    rows = {j: lax.ppermute(pick(j), "x", turn(4, j)) for j in SHIFTS}
    target_block = jnp.stack([pick(0)] + [rows[j] for j in range(1, 4)])
    lines = [target_block] + [lax.ppermute(target_block, "zl", flip(4, k)) for k in range(1, 4)]
    plane = ("y", "c", "x")
    block = jnp.stack([mine, other])
    first = {i: lax.ppermute(block, plane, weave(i, 0)) for i in SHIFTS}
    block = jnp.stack([block] + [first[i] for i in range(1, 4)])
    second = {l: lax.ppermute(block, plane, weave(0, l)) for l in SHIFTS}
    own_core = [block] + [second[l] for l in range(1, 4)]
    other_core = [lax.ppermute(own_core[l], "c", turn(2, 1)) for l in range(4)]
    part = pair_sums(lines, own_core + other_core, exponents, coefficients)
    parts = lax.all_to_all(part, ("zl", "x"), 0, 0, tiled=True)
    return gathered(parts)


def solution(mesh):
    torus = Mesh(mesh.devices.reshape(2, 4, 2, 4, 4), ("zh", "y", "c", "zl", "x"))
    tgt, src = ("zh", "y", "c"), ("zl", "x")
    return jax.shard_map(
        exchange,
        mesh=torus,
        in_specs=(P(tgt, src, None), P(src, tgt, None), P(), P()),
        out_specs=P(src, tgt, None),
        check_vma=False,
    )
```

```python
import jax
import jax.numpy as jnp
import numpy as np
from jax import lax
from jax.experimental import pallas as pl
from jax.experimental.pallas import tpu as pltpu
from jax.sharding import Mesh
from jax.sharding import PartitionSpec as P


G = 64
GAUSS = 8
BF16, F32 = jnp.bfloat16, jnp.float32

SCALE = {0: 1.0, 1: 1.869537353515625, 2: 1.62451171875, 4: 1.13287353515625, 8: 1.8672027587890625, 16: 1.0, 32: 1.0}


def basis():
    n = np.arange(G)
    waves = [(k, np.cos) for k in range(G // 2 + 1)] + [(k, np.sin) for k in range(1, G // 2)]
    rows = np.stack([SCALE[k & -k] * wave(2 * np.pi * k * n / G) for k, wave in waves])
    rows[np.abs(rows) < 1e-12] = 0
    return rows, np.array([k for k, _ in waves])


def basis_blocks():
    rows, _ = basis()
    parity = np.array([2 * r + h for h in range(2) for r in range(32)])
    four = np.eye(4)
    z_in = np.kron(four, rows.T)
    y_in = np.einsum("ky,ab->kbay", rows[:, parity], four).reshape(256, 256)
    x_in = np.einsum("kbx,ij->ikbjx", rows.reshape(G, 16, 4), four).reshape(256, 256)
    twice = lambda m, axis: np.concatenate([m, m], axis=axis)
    return [jnp.asarray(m, BF16) for m in (z_in, twice(y_in, 1), x_in, twice(x_in.T, 1), y_in.T, twice(z_in.T, 0))]


def waves():
    rows, freq = basis()
    table = np.cos(2 * np.pi * np.outer(np.arange(G), freq) / G) / (rows * rows).sum(1)[None]
    return jnp.asarray(np.concatenate([table, table], axis=1), F32)


def spectrum(exponents, coefficients, table, out, outer):
    n = lax.broadcasted_iota(jnp.int32, (GAUSS, G), 1)
    term = lax.broadcasted_iota(jnp.int32, (GAUSS, G), 0)
    distance = jnp.minimum(n, G - n).astype(F32)
    power, weight = jnp.zeros((GAUSS, G), F32), jnp.zeros((GAUSS, G), F32)
    for g in range(GAUSS):
        power = jnp.where(term == g, exponents[g], power)
        weight = jnp.where(term == g, coefficients[g], weight)
    kernel = jnp.exp(-power * (distance * distance))
    weighted = (weight * kernel).astype(BF16).astype(F32)
    kernel = kernel.astype(BF16).astype(F32)
    scaled, plain = jnp.zeros((GAUSS, 128), F32), jnp.zeros((GAUSS, 128), F32)
    for k in range(G):
        row = table[k : k + 1]
        scaled = scaled + weighted[:, k : k + 1] * row
        plain = plain + kernel[:, k : k + 1] * row
    plain = plain.T
    for g in range(GAUSS):
        outer[g] = plain[:40, g : g + 1] * scaled[g : g + 1]
    for k in range(G // 2 + 1):
        total = plain[k : k + 1, 0:1] * outer[0]
        for g in range(1, GAUSS):
            total = total + plain[k : k + 1, g : g + 1] * outer[g]
        for row in (k, G // 2 + k) if 0 < k < G // 2 else (k,):
            out[row, :40] = total
            out[row, 40:] = total[8:32]


def pair_kernel(*refs):
    t_in, s_in = refs[:4], refs[4:12]
    exponents, coefficients, table, z_in, y_in, x_in, x_out, y_out, z_out, out = refs[12:22]
    t_all, s_all, s_rows, field, d_ref, outer = refs[22:]
    zh, y, c, zl, x = (lax.axis_index(a) for a in ("zh", "y", "c", "zl", "x"))
    lane = lax.broadcasted_iota(jnp.int32, (4, 32, 128), 2) < 64

    def swap(a):
        return pltpu.roll(a, 64, 2)

    def by_eights(step):
        def eight(group, carry):
            for n in range(8):
                step(8 * group + n)
            return carry

        lax.fori_loop(0, 2, eight, 0)

    def parts(a, axis):
        high = a.astype(BF16)
        return jnp.concatenate([high, (a - high.astype(F32)).astype(BF16)], axis=axis)

    def dot(a, b):
        return jnp.dot(a, b, preferred_element_type=F32)

    spectrum(exponents, coefficients, table, d_ref, outer)
    for k in range(4):
        for j in range(4):
            t_all[lax.bitwise_xor(zl, k) * 4 + lax.rem(x - j + 4, 4)] = t_in[k][j]

    for e in range(2):
        core = lax.rem(c + e, 2)
        for l in range(4):
            for i in range(4):
                by_x, by_y = i + core * (l - i), l + core * (i - l)
                for m in range(2):
                    b = lax.rem(zh + m, 2) * 8 + lax.rem(y - by_y + 4, 4) * 2 + core
                    s_all[by_x, b] = s_in[4 * e + l][i, m]

    def enter(b):
        target = t_all[b]
        turned = swap(target)
        target = jnp.concatenate([jnp.where(lane, target, turned), jnp.where(lane, turned, target)], axis=1)
        target = target.reshape(256, 128)
        dense = []
        for h in range(2):
            one, two = s_all[2 * h, b], s_all[2 * h + 1, b]
            source = jnp.concatenate([jnp.where(lane, one, swap(two)), jnp.where(lane, swap(one), two)], axis=1)
            source = source.reshape(256, 128)
            s_rows[b, :, 128 * h : 128 * h + 128] = source
            dense.append(target * source)
        along_z = dot(jnp.concatenate(dense, axis=1), z_in[...])
        field[b] = dot(y_in[...], parts(along_z, 0)).astype(BF16)

    by_eights(enter)

    for k in range(16):
        rows = slice(16 * k, 16 * k + 16)
        waves = dot(x_in[...], field[:, rows, :].reshape(256, 256))
        factor = d_ref[4 * k : 4 * k + 4].reshape(256, 128)
        waves = parts(waves * jnp.concatenate([factor, factor], axis=1), 0)
        field[:, rows, :] = dot(x_out[...], waves).astype(BF16).reshape(16, 16, 256)

    def leave(b):
        along_y = parts(dot(y_out[...], field[b]), 1)
        terms = dot(along_y, z_out[...]) * s_rows[b].astype(F32)
        terms = (terms[:, :128] + terms[:, 128:]).reshape(4, G, 128)
        terms = terms + swap(terms)
        out[b] = jnp.where(lane, terms[:, :32], terms[:, 32:]).astype(out.dtype)

    by_eights(leave)


def pair_sums(targets, sources, exponents, coefficients):
    vmem, smem = pl.BlockSpec(memory_space=pltpu.VMEM), pl.BlockSpec(memory_space=pltpu.SMEM)
    return pl.pallas_call(
        pair_kernel,
        out_shape=jax.ShapeDtypeStruct((16, 4, 32, 128), BF16),
        in_specs=[vmem] * 12 + [smem] * 2 + [vmem] * 7,
        out_specs=vmem,
        scratch_shapes=[
            pltpu.VMEM((16, 4, 32, 128), BF16),
            pltpu.VMEM((4, 16, 4, 32, 128), BF16),
            pltpu.VMEM((16, 256, 256), BF16),
            pltpu.VMEM((16, 256, 256), BF16),
            pltpu.VMEM((G, G, 128), F32),
            pltpu.VMEM((GAUSS, 40, 128), F32),
        ],
        compiler_params=pltpu.CompilerParams(vmem_limit_bytes=24 << 20),
    )(*targets, *sources, exponents, coefficients, waves(), *basis_blocks())


def gather_kernel(parts, out, rows):
    for t in range(4):
        total = parts[t].astype(F32)
        for q in range(1, 4):
            total = total + parts[4 * q + t].astype(F32)
        rows[128 * t : 128 * t + 128] = -total.reshape(128, 128)
    for p in range(4):
        for r in range(32):
            out[p, :, 128 * r : 128 * r + 128] = rows[pl.ds(32 * p + r, 4, stride=128)]


def gathered(parts):
    vmem = pl.BlockSpec(memory_space=pltpu.VMEM)
    return pl.pallas_call(
        gather_kernel,
        out_shape=jax.ShapeDtypeStruct((4, 4, G * G), F32),
        in_specs=[vmem],
        out_specs=vmem,
        scratch_shapes=[pltpu.VMEM((512, 128), F32)],
        compiler_params=pltpu.CompilerParams(vmem_limit_bytes=8 << 20),
    )(parts)


def turn(n, by):
    return [(i, (i + by) % n) for i in range(n)]


def flip(n, by):
    return [(i, i ^ by) for i in range(n)]


def weave(along_x, along_y):
    place = lambda y, c, x: ((y % 4) * 2 + c) * 4 + x % 4
    pairs = []
    for y in range(4):
        for x in range(4):
            pairs.append((place(y, 0, x), place(y + along_y, 0, x + along_x)))
            pairs.append((place(y, 1, x), place(y + along_x, 1, x + along_y)))
    return pairs


SHIFTS = (2, 1, 3)


def exchange(targets, sources, exponents, coefficients):
    x = lax.axis_index("x")
    mine = sources.reshape(4, 32, 128)
    other = lax.ppermute(mine, "zh", turn(2, 1))
    packed = targets.reshape(4, 4, 32, 128)
    pick = lambda j: lax.dynamic_index_in_dim(packed, (x + j) % 4, 0, keepdims=False)
    rows = {j: lax.ppermute(pick(j), "x", turn(4, j)) for j in SHIFTS}
    target_block = jnp.stack([pick(0)] + [rows[j] for j in range(1, 4)])
    lines = [target_block] + [lax.ppermute(target_block, "zl", flip(4, k)) for k in range(1, 4)]
    plane = ("y", "c", "x")
    block = jnp.stack([mine, other])
    first = {i: lax.ppermute(block, plane, weave(i, 0)) for i in SHIFTS}
    block = jnp.stack([block] + [first[i] for i in range(1, 4)])
    second = {l: lax.ppermute(block, plane, weave(0, l)) for l in SHIFTS}
    own_core = [block] + [second[l] for l in range(1, 4)]
    other_core = [lax.ppermute(own_core[l], "c", turn(2, 1)) for l in range(4)]
    part = pair_sums(lines, own_core + other_core, exponents, coefficients)
    parts = lax.all_to_all(part, ("zl", "x"), 0, 0, tiled=True)
    return gathered(parts)


def solution(mesh):
    torus = Mesh(mesh.devices.reshape(2, 4, 2, 4, 4), ("zh", "y", "c", "zl", "x"))
    tgt, src = ("zh", "y", "c"), ("zl", "x")
    return jax.shard_map(
        exchange,
        mesh=torus,
        in_specs=(P(tgt, src, None), P(src, tgt, None), P(), P()),
        out_specs=P(src, tgt, None),
        check_vma=False,
    )
```
